32 devices in a mesh: gy: 8 (over z, x), gz: 4 (over y, core).
Axes of the slice: x: 2, y: 2, z: 4, core: 2. Of those that a mesh axis runs over, the one named last changes fastest.
Arguments:
- tokens: bfloat16 [16, 64, 16, 192], P(None, 'gy', 'gz'), may hold values from -36 to 36
- qkv_weight: bfloat16 [192, 576], replicated, may hold values from -0.4375 to 0.4375
- out_weight: bfloat16 [192, 192], replicated, may hold values from -1.25 to 1.25
- conv_kernel: float32 [3, 3, 3, 192], replicated, may hold values from -1.25 to 1.25
- up_weight: bfloat16 [192, 768], replicated, may hold values from -0.4375 to 0.4375
- down_weight: bfloat16 [768, 192], replicated, may hold values from -0.21875 to 0.21875
- band_mask: int32 [4, 4], replicated, may hold values from 0 to 1, as said below
- grad_out: bfloat16 [16, 64, 16, 192], P(None, 'gy', 'gz'), may hold values from -6 to 6
Outputs:
- block_out: bfloat16 [16, 64, 16, 192], P(None, 'gy', 'gz')
- token_gradient: bfloat16 [16, 64, 16, 192], P(None, 'gy', 'gz')
- qkv_gradient: float32 [192, 576], replicated
- out_gradient: float32 [192, 192], replicated
- kernel_gradient: float32 [3, 3, 3, 192], replicated
- up_gradient: float32 [192, 768], replicated
- down_gradient: float32 [768, 192], replicated
The draws below stay inside these ranges and needn't reach their ends.
Inputs may be any that keep to these rules, and one draw needn't show every extreme that they name: band_mask[i, i] is 1, and band_mask[i, j] is 0 where |i - j| > 4; other entries are 0 or 1.
All inputs are finite; a program needn't handle non-finite values.
Results may differ from the reference program's by a relative error of at most 0.017.
Values may be sent and summed in bfloat16 or wider, within the bound.
A program may use at most 64 MiB of HBM per device.

```python
import math
import jax
import jax.numpy as jnp
from jax import lax

C = 192
HEADS = 6
F = 768
BLOCK = 16
BAND = 4
X = 16
Y = 64
Z = 16
NBY = 4


def draw_tokens(key, part):
    noise_key, row_key, column_key = jax.random.split(key, 3)
    column_scale = jnp.exp(jax.random.uniform(column_key, (C,), jnp.float32, math.log(0.3), math.log(3.0)))
    noise_field = jax.random.truncated_normal(noise_key, -4.0, 4.0, (X, Y, Z, C), jnp.float32)
    row_scale = jnp.exp(jax.random.uniform(row_key, (X, Y, Z, 1), jnp.float32, math.log(0.3), math.log(3.0)))
    token_field = noise_field * row_scale * column_scale
    return token_field.astype(jnp.bfloat16)


def draw_band_mask(key, part):
    rows_index = jnp.arange(NBY, dtype=jnp.int32)[:, None]
    cols_index = jnp.arange(NBY, dtype=jnp.int32)[None, :]
    distance = jnp.abs(rows_index - cols_index)
    coin_flips = jax.random.randint(key, (NBY, NBY), 0, 4, dtype=jnp.int32)
    kept_blocks = jnp.where(coin_flips > 0, 1, 0)
    return jnp.where(distance == 0, 1, jnp.where(distance <= BAND, kept_blocks, 0)).astype(jnp.int32)


def shard_levels(key, shape, cuts, smallest, largest):
    loudness = 1.0
    for position, parts in cuts:
        draws = jax.random.uniform(jax.random.fold_in(jax.random.fold_in(key, 6), position), (parts,), jnp.float32, smallest / len(cuts), largest / len(cuts))
        loudness = loudness * jnp.repeat(jnp.exp(draws), shape[position] // parts).reshape((-1,) + (1,) * (len(shape) - 1 - position))
    return loudness


def bell_draw(key, shape, spread, most, cuts=(), kind=jnp.bfloat16):
    loudness = shard_levels(key, shape, cuts, -0.22, 0.18) if cuts else 1.0
    result = jax.random.normal(key, shape, jnp.float32) * spread * loudness
    return jnp.minimum(jnp.maximum(result, -most), most).astype(kind)


def setup_inputs(seed: int = 0) -> dict:
    key_list = jax.random.split(jax.random.key(seed), 9)
    return {
        "tokens": draw_tokens(jax.random.fold_in(key_list[8], 71), 0),
        "qkv_weight": bell_draw(key_list[1], (C, 3 * C), C ** -0.5, 0.4375),
        "out_weight": bell_draw(key_list[2], (C, C), (C // 8) ** -0.5, 1.25),
        "conv_kernel": bell_draw(key_list[3], (3, 3, 3, C), 27 ** -0.5, 1.25, (), jnp.float32),
        "up_weight": bell_draw(key_list[4], (C, F), C ** -0.5, 0.4375),
        "down_weight": bell_draw(key_list[5], (F, C), F ** -0.5, 0.21875),
        "band_mask": draw_band_mask(jax.random.fold_in(key_list[8], 71), 0),
        "grad_out": bell_draw(key_list[7], (X, Y, Z, C), 1.0, 6.0, ((1, 8), (2, 4))),
    }


NORM_EPS = 1e-05
UNIT_EPS = 1e-06
GELU_SLOPE = 0.7978845608028654
GELU_CUBIC = 0.044715

def norm_rows(values):
    centred = values - lax.optimization_barrier(jnp.mean(values, axis=-1, keepdims=True))
    inverse = lax.rsqrt(lax.optimization_barrier(jnp.mean(centred * centred, axis=-1, keepdims=True)) + NORM_EPS)
    return (centred * inverse, inverse)

def norm_rows_back(upstream, normal, inverse):
    return inverse * (upstream - lax.optimization_barrier(jnp.mean(upstream, axis=-1, keepdims=True)) - normal * lax.optimization_barrier(jnp.mean(upstream * normal, axis=-1, keepdims=True)))

def unit_scale(values):
    return lax.rsqrt(lax.optimization_barrier(jnp.mean(values * values, axis=-1, keepdims=True)) + UNIT_EPS)

def unit_back(upstream, values, scaling):
    return scaling * upstream - scaling * scaling * scaling * values * lax.optimization_barrier(jnp.mean(upstream * values, axis=-1, keepdims=True))

def gelu_value(pre_act):
    return 0.5 * pre_act * (1.0 + jnp.tanh(GELU_SLOPE * (pre_act + GELU_CUBIC * pre_act * pre_act * pre_act)))

def gelu_slope(pre_act):
    tangent = jnp.tanh(GELU_SLOPE * (pre_act + GELU_CUBIC * pre_act * pre_act * pre_act))
    return 0.5 * (1.0 + tangent) + 0.5 * pre_act * (1.0 - tangent * tangent) * GELU_SLOPE * (1.0 + 3.0 * GELU_CUBIC * pre_act * pre_act)

def flatten_rows(values):
    return values.reshape(-1, values.shape[-1])

def project(values, weight):
    summed = jnp.dot(flatten_rows(values), weight, preferred_element_type=jnp.float32)
    return summed.reshape(values.shape[:-1] + (weight.shape[1],))

def project_back(values, weight):
    summed = lax.dot_general(flatten_rows(values), weight, (((1,), (1,)), ((), ())), preferred_element_type=jnp.float32)
    return summed.reshape(values.shape[:-1] + (weight.shape[0],))

def contract(left_rows, right_rows):
    return lax.dot_general(flatten_rows(left_rows), flatten_rows(right_rows), (((0,), (0,)), ((), ())), preferred_element_type=jnp.float32)

def split_heads(values, head_count):
    return values.reshape(values.shape[:-1] + (head_count, values.shape[-1] // head_count))

def join_heads(values):
    return values.reshape(values.shape[:-2] + (values.shape[-2] * values.shape[-1],))

def head_product(einsum_form, left_side, right_side):
    return jnp.einsum(einsum_form, left_side.astype(jnp.float32), right_side.astype(jnp.float32))

def attention_parts(qkv_rows, mask_full, head_count):
    feature_width = qkv_rows.shape[-1] // 3
    query_vec = qkv_rows[..., :feature_width].astype(jnp.float32)
    key_vec = qkv_rows[..., feature_width:2 * feature_width].astype(jnp.float32)
    query_scale = unit_scale(query_vec)
    key_scale = unit_scale(key_vec)
    query_unit = (query_vec * query_scale).astype(jnp.bfloat16)
    key_unit = (key_vec * key_scale).astype(jnp.bfloat16)
    factor = 2.0 / math.sqrt(feature_width // head_count)
    scores = head_product('aibhd,ajbhd->abhij', split_heads(query_unit, head_count), split_heads(key_unit, head_count))
    weights = mask_full * jnp.exp(factor * scores)
    attn_probs = weights / lax.optimization_barrier(jnp.sum(weights, axis=-1, keepdims=True))
    return (query_vec, key_vec, query_scale, key_scale, query_unit, key_unit, attn_probs, factor)

def attend(qkv_rows, mask_full, head_count):
    query_vec, key_vec, query_scale, key_scale, query_unit, key_unit, attn_probs, factor = attention_parts(qkv_rows, mask_full, head_count)
    feature_width = qkv_rows.shape[-1] // 3
    value_heads = split_heads(qkv_rows[..., 2 * feature_width:], head_count)
    probs_low = attn_probs.astype(jnp.bfloat16)
    mixed_heads = head_product('abhij,ajbhd->aibhd', probs_low, value_heads)
    return join_heads(mixed_heads).astype(jnp.bfloat16)

def attend_back(qkv_rows, mask_full, head_count, upstream):
    query_vec, key_vec, query_scale, key_scale, query_unit, key_unit, attn_probs, factor = attention_parts(qkv_rows, mask_full, head_count)
    feature_width = qkv_rows.shape[-1] // 3
    value_heads = split_heads(qkv_rows[..., 2 * feature_width:], head_count)
    grad_heads = split_heads(upstream, head_count)
    probs_low = attn_probs.astype(jnp.bfloat16)
    grad_probs = head_product('aibhd,ajbhd->abhij', grad_heads, value_heads)
    grad_values = head_product('abhij,aibhd->ajbhd', probs_low, grad_heads)
    grad_scores = attn_probs * (grad_probs - lax.optimization_barrier(jnp.sum(grad_probs * attn_probs, axis=-1, keepdims=True)))
    grad_low = (factor * grad_scores).astype(jnp.bfloat16)
    grad_qunit = join_heads(head_product('abhij,ajbhd->aibhd', grad_low, split_heads(key_unit, head_count)))
    grad_kunit = join_heads(head_product('abhij,aibhd->ajbhd', grad_low, split_heads(query_unit, head_count)))
    grad_query = unit_back(grad_qunit, query_vec, query_scale).astype(jnp.bfloat16)
    grad_key = unit_back(grad_kunit, key_vec, key_scale).astype(jnp.bfloat16)
    return jnp.concatenate([grad_query, grad_key, join_heads(grad_values).astype(jnp.bfloat16)], axis=-1)

def conv_apply(padded, kernel_taps):
    extent_x = padded.shape[0] - 2
    extent_y = padded.shape[1] - 2
    extent_z = padded.shape[2] - 2
    summed = jnp.zeros((extent_x, extent_y, extent_z, padded.shape[3]), jnp.float32)
    for shift_x in range(3):
        for shift_y in range(3):
            for shift_z in range(3):
                window = padded[shift_x:shift_x + extent_x, shift_y:shift_y + extent_y, shift_z:shift_z + extent_z]
                summed = summed + kernel_taps[shift_x, shift_y, shift_z] * window.astype(jnp.float32)
    return summed

def kernel_grad(padded, upstream):
    extent_x, extent_y, extent_z, channels = upstream.shape
    upstream_wide = upstream.astype(jnp.float32)
    pieces = []
    for shift_x in range(3):
        for shift_y in range(3):
            for shift_z in range(3):
                window = padded[shift_x:shift_x + extent_x, shift_y:shift_y + extent_y, shift_z:shift_z + extent_z]
                pieces.append(lax.optimization_barrier(jnp.sum(window.astype(jnp.float32) * upstream_wide, axis=(0, 1, 2))))
    return jnp.stack(pieces).reshape(3, 3, 3, channels)

def mlp_pass(mixed_field, upstream, up_weight, down_weight):
    mixed_wide = mixed_field.astype(jnp.float32)
    normal, inverse = norm_rows(mixed_wide)
    normed = normal.astype(jnp.bfloat16)
    pre_act = project(normed, up_weight)
    hidden = gelu_value(pre_act).astype(jnp.bfloat16)
    block_out = (mixed_wide + project(hidden, down_weight)).astype(jnp.bfloat16)
    grad_hidden = project_back(upstream, down_weight).astype(jnp.bfloat16)
    part_down = contract(hidden, upstream)
    grad_pre = (grad_hidden.astype(jnp.float32) * gelu_slope(pre_act)).astype(jnp.bfloat16)
    part_up = contract(normed, grad_pre)
    grad_normed = project_back(grad_pre, up_weight)
    grad_mixed = (upstream.astype(jnp.float32) + norm_rows_back(grad_normed, normal, inverse)).astype(jnp.bfloat16)
    return (block_out, grad_mixed, part_up, part_down)

def pad_box(field_values):
    wrapped = jnp.pad(field_values, ((0, 0), (1, 1), (1, 1), (0, 0)), mode='wrap')
    return jnp.pad(wrapped, ((1, 1), (0, 0), (0, 0), (0, 0)))

def reference(tokens, qkv_weight, out_weight, conv_kernel, up_weight, down_weight, band_mask, grad_out):
    block_count = band_mask.shape[0]
    line_length = block_count * BLOCK
    mask_full = jnp.broadcast_to(band_mask[:, None, :, None], (block_count, BLOCK, block_count, BLOCK)).reshape(line_length, line_length).astype(jnp.float32)
    flipped = conv_kernel[::-1, ::-1, ::-1]

    def forward_slab(token_slab):
        token_wide = token_slab[None].astype(jnp.float32)
        normal, inverse = norm_rows(token_wide)
        normed = normal.astype(jnp.bfloat16)
        qkv_rows = project(normed, qkv_weight).astype(jnp.bfloat16)
        attended = attend(qkv_rows, mask_full, HEADS)
        return (token_wide + project(attended, out_weight)).astype(jnp.bfloat16)[0]
    value_field = lax.map(forward_slab, tokens)
    padded_value = pad_box(value_field)
    channels = tokens.shape[3]

    def mlp_slab(running, plane_index):
        window = lax.dynamic_slice_in_dim(padded_value, plane_index, 3, 0)
        centre = lax.dynamic_slice_in_dim(value_field, plane_index, 1, 0)
        mixed_field = (centre.astype(jnp.float32) + conv_apply(window, conv_kernel)).astype(jnp.bfloat16)
        upstream = lax.dynamic_slice_in_dim(grad_out, plane_index, 1, 0)
        block_out, grad_mixed, part_up, part_down = mlp_pass(mixed_field, upstream, up_weight, down_weight)
        return ((running[0] + part_up, running[1] + part_down), (block_out[0], grad_mixed[0]))
    start_up = jnp.zeros(up_weight.shape, jnp.float32)
    start_down = jnp.zeros(down_weight.shape, jnp.float32)
    plane_list = jnp.arange(X, dtype=jnp.int32)
    sums_mlp, slabs_mlp = lax.scan(mlp_slab, (start_up, start_down), plane_list)
    block_out_all, grad_mixed_all = slabs_mlp
    padded_grad = pad_box(grad_mixed_all)

    def back_slab(running, plane_index):
        grad_window = lax.dynamic_slice_in_dim(padded_grad, plane_index, 3, 0)
        value_window = lax.dynamic_slice_in_dim(padded_value, plane_index, 3, 0)
        grad_centre = lax.dynamic_slice_in_dim(grad_mixed_all, plane_index, 1, 0)
        grad_value = (grad_centre.astype(jnp.float32) + conv_apply(grad_window, flipped)).astype(jnp.bfloat16)
        part_kernel = kernel_grad(value_window, grad_centre)
        token_slab = lax.dynamic_slice_in_dim(tokens, plane_index, 1, 0)
        token_wide = token_slab.astype(jnp.float32)
        normal, inverse = norm_rows(token_wide)
        normed = normal.astype(jnp.bfloat16)
        qkv_rows = project(normed, qkv_weight).astype(jnp.bfloat16)
        attended = attend(qkv_rows, mask_full, HEADS)
        grad_attended = project_back(grad_value, out_weight).astype(jnp.bfloat16)
        part_out = contract(attended, grad_value)
        grad_qkv = attend_back(qkv_rows, mask_full, HEADS, grad_attended)
        grad_normed = project_back(grad_qkv, qkv_weight).astype(jnp.bfloat16)
        part_qkv = contract(normed, grad_qkv)
        grad_token = (grad_value.astype(jnp.float32) + norm_rows_back(grad_normed.astype(jnp.float32), normal, inverse)).astype(jnp.bfloat16)
        return ((running[0] + part_qkv, running[1] + part_out, running[2] + part_kernel), grad_token[0])
    start_qkv = jnp.zeros(qkv_weight.shape, jnp.float32)
    start_out = jnp.zeros(out_weight.shape, jnp.float32)
    start_kernel = jnp.zeros((3, 3, 3, channels), jnp.float32)
    sums_back, token_gradient = lax.scan(back_slab, (start_qkv, start_out, start_kernel), plane_list)
    factor = 1.0 / math.sqrt(X * Y * Z)
    return (block_out_all, token_gradient, sums_back[0] * factor, sums_back[1] * factor, sums_back[2] * factor, sums_mlp[0] * factor, sums_mlp[1] * factor)
```

```python
import functools
import math

import jax
import jax.numpy as jnp
from jax import lax
from jax.experimental import pallas as pl
from jax.experimental.pallas import tpu as pltpu
from jax.sharding import PartitionSpec as P

HEADS = 6
BLOCK = 16


NORM_EPS = 1e-05
UNIT_EPS = 1e-06
GELU_SLOPE = 0.7978845608028654
GELU_CUBIC = 0.044715


def norm_rows(values):
    centred = values - jnp.mean(values, axis=-1, keepdims=True)
    inverse = lax.rsqrt(jnp.mean(centred * centred, axis=-1, keepdims=True) + NORM_EPS)
    return (centred * inverse, inverse)


def norm_rows_back(upstream, normal, inverse):
    return inverse * (
        upstream
        - jnp.mean(upstream, axis=-1, keepdims=True)
        - normal * jnp.mean(upstream * normal, axis=-1, keepdims=True)
    )


def unit_scale(values):
    return lax.rsqrt(jnp.mean(values * values, axis=-1, keepdims=True) + UNIT_EPS)


def unit_back(upstream, values, scaling):
    return scaling * upstream - scaling * scaling * scaling * values * jnp.mean(
        upstream * values, axis=-1, keepdims=True
    )


def gelu_value(pre_act):
    return (
        0.5
        * pre_act
        * (1.0 + jnp.tanh(GELU_SLOPE * (pre_act + GELU_CUBIC * pre_act * pre_act * pre_act)))
    )


def gelu_slope(pre_act):
    tangent = jnp.tanh(GELU_SLOPE * (pre_act + GELU_CUBIC * pre_act * pre_act * pre_act))
    return 0.5 * (1.0 + tangent) + 0.5 * pre_act * (1.0 - tangent * tangent) * GELU_SLOPE * (
        1.0 + 3.0 * GELU_CUBIC * pre_act * pre_act
    )


def flatten_rows(values):
    return values.reshape(-1, values.shape[-1])


def project(values, weight):
    summed = jnp.dot(flatten_rows(values), weight, preferred_element_type=jnp.float32)
    return summed.reshape(values.shape[:-1] + (weight.shape[1],))


def project_back(values, weight):
    summed = lax.dot_general(
        flatten_rows(values), weight, (((1,), (1,)), ((), ())), preferred_element_type=jnp.float32
    )
    return summed.reshape(values.shape[:-1] + (weight.shape[0],))


def contract(left_rows, right_rows):
    return lax.dot_general(
        flatten_rows(left_rows),
        flatten_rows(right_rows),
        (((0,), (0,)), ((), ())),
        preferred_element_type=jnp.float32,
    )


def split_heads(values, head_count):
    return values.reshape(values.shape[:-1] + (head_count, values.shape[-1] // head_count))


def join_heads(values):
    return values.reshape(values.shape[:-2] + (values.shape[-2] * values.shape[-1],))


def head_product(einsum_form, left_side, right_side):
    return jnp.einsum(einsum_form, left_side, right_side, preferred_element_type=jnp.float32)


MESH = pl.DeviceIdType.MESH
VMEM = pl.BlockSpec(memory_space=pltpu.VMEM)


def greet(peers):
    barrier = pltpu.get_barrier_semaphore()
    for peer in peers:
        pl.semaphore_signal(barrier, inc=1, device_id=peer, device_id_type=MESH)
    pl.semaphore_wait(barrier, len(peers))


def line_peers(count):
    me_y, me_z = lax.axis_index("gy"), lax.axis_index("gz")
    return [(lax.rem(me_y + k, count), me_z) for k in range(1, count)]


def swap_copies(count, pairs, send_sem, recv_sem):
    me_y, me_z = lax.axis_index("gy"), lax.axis_index("gz")
    copies = []
    for k in range(1, count):
        peer = lax.rem(me_y + k, count)
        for a, (source, target) in enumerate(pairs):
            copies.append(
                pltpu.make_async_remote_copy(
                    src_ref=source.at[peer],
                    dst_ref=target.at[me_y],
                    send_sem=send_sem.at[a, k],
                    recv_sem=recv_sem.at[a, k],
                    device_id=(peer, me_z),
                    device_id_type=MESH,
                )
            )
    return copies


def swap_kernel(count, first_in, second_in, first_out, second_out, send_sem, recv_sem):
    greet(line_peers(count))
    pairs = ((first_in, first_out), (second_in, second_out))
    copies = swap_copies(count, pairs, send_sem, recv_sem)
    for copy in copies:
        copy.start()
    me_y = lax.axis_index("gy")
    for source, target in pairs:
        target[me_y] = source[me_y]
    for copy in copies:
        copy.wait()


def swap_lines(first, second, count):
    shape = jax.ShapeDtypeStruct(first.shape, first.dtype)
    return pl.pallas_call(
        functools.partial(swap_kernel, count),
        out_shape=(shape, shape),
        in_specs=[VMEM, VMEM],
        out_specs=(VMEM, VMEM),
        scratch_shapes=[pltpu.SemaphoreType.DMA((2, count)), pltpu.SemaphoreType.DMA((2, count))],
        compiler_params=pltpu.CompilerParams(collective_id=0, has_side_effects=True),
        name="swap_lines",
    )(first, second)


def face(step, extent):
    return {0: (pl.ds(0, extent), pl.ds(1, extent)), 1: (pl.ds(extent - 1, 1), pl.ds(0, 1)), -1: (pl.ds(0, 1), pl.ds(extent + 1, 1))}[step]


def halo_kernel(count_y, count_z, cells, padded, send_sem, recv_sem):
    me_y, me_z = lax.axis_index("gy"), lax.axis_index("gz")
    extent_x, extent_z = cells.shape[0], cells.shape[1]
    steps = [(dx, dz) for dx in (-1, 0, 1) for dz in (-1, 0, 1) if (dx, dz) != (0, 0)]
    barrier = pltpu.get_barrier_semaphore()

    def reach(dx, action):
        if dx == 0:
            action()
        elif dx == 1:
            pl.when(me_y < count_y - 1)(action)
        else:
            pl.when(me_y > 0)(action)

    def place(dx, dz):
        return (me_y + dx, lax.rem(me_z + dz + count_z, count_z))

    def greet_one(dx, dz):
        pl.semaphore_signal(barrier, inc=1, device_id=place(dx, dz), device_id_type=MESH)

    for dx, dz in steps:
        reach(dx, functools.partial(greet_one, dx, dz))
    inner = (me_y > 0) & (me_y < count_y - 1)

    @pl.when(inner)
    def _():
        pl.semaphore_wait(barrier, 8)

    @pl.when(jnp.logical_not(inner))
    def _():
        pl.semaphore_wait(barrier, 5)

    def copy_of(index):
        dx, dz = steps[index]
        from_x, to_x = face(dx, extent_x)
        from_z, to_z = face(dz, extent_z)
        return pltpu.make_async_remote_copy(
            src_ref=cells.at[from_x, from_z],
            dst_ref=padded.at[to_x, to_z],
            send_sem=send_sem.at[index],
            recv_sem=recv_sem.at[index],
            device_id=place(dx, dz),
            device_id_type=MESH,
        )

    for index, (dx, dz) in enumerate(steps):
        reach(dx, lambda index=index: copy_of(index).start())
    padded[1 : extent_x + 1, 1 : extent_z + 1] = cells[...]
    blank = jnp.zeros((1,) + tuple(padded.shape[1:]), padded.dtype)

    @pl.when(me_y == 0)
    def _():
        padded[0:1] = blank

    @pl.when(me_y == count_y - 1)
    def _():
        padded[extent_x + 1 : extent_x + 2] = blank

    for index, (dx, dz) in enumerate(steps):
        reach(dx, lambda index=index: copy_of(index).wait_send())
        reach(-dx, lambda index=index: copy_of(index).wait_recv())


def halo(cells, count_y, count_z, number):
    shape = (cells.shape[0] + 2, cells.shape[1] + 2) + cells.shape[2:]
    return pl.pallas_call(
        functools.partial(halo_kernel, count_y, count_z),
        out_shape=jax.ShapeDtypeStruct(shape, cells.dtype),
        in_specs=[VMEM],
        out_specs=VMEM,
        scratch_shapes=[pltpu.SemaphoreType.DMA((8,)), pltpu.SemaphoreType.DMA((8,))],
        compiler_params=pltpu.CompilerParams(collective_id=number, has_side_effects=True),
        name="halo%d" % number,
    )(cells)


def bits_of(count_y, count_z):
    levels = []
    for axis, count in (("gz", count_z), ("gy", count_y)):
        bit = 1
        while bit < count:
            levels.append((axis, bit))
            bit *= 2
    return levels


def reduce_kernel(count_y, count_z, parts, first_in, second_in, sums, first_out, second_out, *scratch):
    swap_send, swap_recv, send_sem, recv_sem, total = scratch[:5]
    stages = bits_of(count_y, count_z)
    depth = len(stages)
    outgoing, incoming = scratch[5 : 5 + depth], scratch[5 + depth : 5 + 2 * depth]
    me = {"gy": lax.axis_index("gy"), "gz": lax.axis_index("gz")}
    bit_values, partners = [], []
    for axis, bit in stages:
        value = lax.rem(me[axis] // bit, 2)
        moved = me[axis] + bit * (1 - 2 * value)
        bit_values.append(value)
        partners.append((moved, me["gz"]) if axis == "gy" else (me["gy"], moved))
    greet(line_peers(count_y) + [partner for (axis, _), partner in zip(stages, partners) if axis == "gz"])
    pairs = ((first_in, first_out), (second_in, second_out))
    copies = swap_copies(count_y, pairs, swap_send, swap_recv)
    for copy in copies:
        copy.start()
    for source, target in pairs:
        target[me["gy"]] = source[me["gy"]]
    held, size = parts, parts.shape[0]
    base, bases = 0, []
    for level in range(depth):
        half = size // 2
        keep = base + bit_values[level] * half
        away = base + (1 - bit_values[level]) * half
        outgoing[level][...] = held[pl.ds(away, half)].astype(jnp.bfloat16)
        copy = pltpu.make_async_remote_copy(
            src_ref=outgoing[level],
            dst_ref=incoming[level],
            send_sem=send_sem.at[level],
            recv_sem=recv_sem.at[level],
            device_id=partners[level],
            device_id_type=MESH,
        )
        copy.start()
        copy.wait()
        total[pl.ds(keep, half)] = held[pl.ds(keep, half)] + incoming[level][...].astype(jnp.float32)
        held, base, size = total, keep, half
        bases.append(keep)
    sums[pl.ds(base, size)] = total[pl.ds(base, size)].astype(jnp.bfloat16)
    for level in range(depth - 1, -1, -1):
        span = pl.ds(bases[level], size)
        copy = pltpu.make_async_remote_copy(
            src_ref=sums.at[span],
            dst_ref=sums.at[span],
            send_sem=send_sem.at[depth + level],
            recv_sem=recv_sem.at[depth + level],
            device_id=partners[level],
            device_id_type=MESH,
        )
        copy.start()
        copy.wait()
        size *= 2
    for copy in copies:
        copy.wait()


def reduce_and_swap(parts, first, second, count_y, count_z):
    depth = len(bits_of(count_y, count_z))
    shape = jax.ShapeDtypeStruct(first.shape, first.dtype)
    halves = [
        pltpu.VMEM((parts.shape[0] >> (level + 1),) + parts.shape[1:], jnp.bfloat16)
        for level in range(depth)
    ]
    return pl.pallas_call(
        functools.partial(reduce_kernel, count_y, count_z),
        out_shape=(jax.ShapeDtypeStruct(parts.shape, jnp.bfloat16), shape, shape),
        in_specs=[VMEM, VMEM, VMEM],
        out_specs=(VMEM, VMEM, VMEM),
        scratch_shapes=[
            pltpu.SemaphoreType.DMA((2, count_y)),
            pltpu.SemaphoreType.DMA((2, count_y)),
            pltpu.SemaphoreType.DMA((2 * depth,)),
            pltpu.SemaphoreType.DMA((2 * depth,)),
            pltpu.VMEM(parts.shape, jnp.float32),
        ]
        + halves
        + halves,
        compiler_params=pltpu.CompilerParams(
            collective_id=3, has_side_effects=True, vmem_limit_bytes=24 * 1024 * 1024
        ),
        name="reduce_and_swap",
    )(parts, first, second)


def tiles_of(matrix):
    rows, columns = matrix.shape
    return (
        matrix.reshape(rows // 16, 16, columns // 128, 128)
        .transpose(0, 2, 1, 3)
        .reshape(-1, 16, 128)
    )


def from_tiles(tiles, rows, columns):
    return (
        tiles.reshape(rows // 16, columns // 128, 16, 128)
        .transpose(0, 2, 1, 3)
        .reshape(rows, columns)
    )


def to_lines(swapped, extents):
    planes, part_y, part_z, width = extents
    lines = swapped.reshape(-1, planes, part_y, part_z, width).transpose(1, 3, 0, 2, 4)
    return lines.reshape(planes, part_z, -1, width)


def from_lines(lines, extents):
    planes, part_y, part_z, width = extents
    split = lines.reshape(planes, part_z, -1, part_y, width).transpose(2, 0, 3, 1, 4)
    return split.reshape(split.shape[0], -1, width)

def attention_parts(qkv_rows, mask_full, head_count):
    feature_width = qkv_rows.shape[-1] // 3
    query_vec = qkv_rows[..., :feature_width].astype(jnp.float32)
    key_vec = qkv_rows[..., feature_width : 2 * feature_width].astype(jnp.float32)
    query_scale = unit_scale(query_vec)
    key_scale = unit_scale(key_vec)
    query_unit = (query_vec * query_scale).astype(jnp.bfloat16)
    key_unit = (key_vec * key_scale).astype(jnp.bfloat16)
    factor = 2.0 / math.sqrt(feature_width // head_count)
    scores = head_product(
        "abihd,abjhd->abhij", split_heads(query_unit, head_count), split_heads(key_unit, head_count)
    )
    weights = mask_full * jnp.exp(factor * scores)
    attn_probs = weights / jnp.sum(weights, axis=-1, keepdims=True)
    return (query_vec, key_vec, query_scale, key_scale, query_unit, key_unit, attn_probs, factor)


def attention_forward(token_lines, qkv_weight, out_weight, mask_full):
    token_wide = token_lines.astype(jnp.float32)
    normal, inverse = norm_rows(token_wide)
    normed = normal.astype(jnp.bfloat16)
    qkv_rows = project(normed, qkv_weight).astype(jnp.bfloat16)
    parts = attention_parts(qkv_rows, mask_full, HEADS)
    width = token_lines.shape[-1]
    value_heads = split_heads(qkv_rows[..., 2 * width :], HEADS)
    probs_low = parts[6].astype(jnp.bfloat16)
    attended = join_heads(head_product("abhij,abjhd->abihd", probs_low, value_heads)).astype(
        jnp.bfloat16
    )
    value_field = (token_wide + project(attended, out_weight)).astype(jnp.bfloat16)
    return value_field, (qkv_rows, attended)


def conv_apply(padded, kernel_taps):
    grown = jnp.concatenate([padded[:, :, -1:], padded, padded[:, :, :1]], axis=2)
    extent_x, extent_z, extent_y = padded.shape[0] - 2, padded.shape[1] - 2, padded.shape[2]
    summed = jnp.zeros((extent_x, extent_z, extent_y, padded.shape[3]), jnp.float32)
    for a in range(3):
        for b in range(3):
            for d in range(3):
                window = grown[a : a + extent_x, d : d + extent_z, b : b + extent_y]
                summed = summed + kernel_taps[a, b, d] * window.astype(jnp.float32)
    return summed


def kernel_grad(padded, upstream):
    grown = jnp.concatenate([padded[:, :, -1:], padded, padded[:, :, :1]], axis=2)
    extent_x, extent_z, extent_y, channels = upstream.shape
    upstream_wide = upstream.astype(jnp.float32)
    pieces = []
    for a in range(3):
        for b in range(3):
            for d in range(3):
                window = grown[a : a + extent_x, d : d + extent_z, b : b + extent_y]
                pieces.append(jnp.sum(window.astype(jnp.float32) * upstream_wide, axis=(0, 1, 2)))
    return jnp.stack(pieces)


def feed_forward(padded_value, upstream, conv_kernel, up_weight, down_weight):
    value_field = padded_value[1:-1, 1:-1]
    mixed_field = (value_field.astype(jnp.float32) + conv_apply(padded_value, conv_kernel)).astype(
        jnp.bfloat16
    )
    mixed_wide = mixed_field.astype(jnp.float32)
    normal, inverse = norm_rows(mixed_wide)
    normed = normal.astype(jnp.bfloat16)
    pre_act = project(normed, up_weight)
    hidden = gelu_value(pre_act).astype(jnp.bfloat16)
    block_out = (mixed_wide + project(hidden, down_weight)).astype(jnp.bfloat16)
    grad_hidden = project_back(upstream, down_weight).astype(jnp.bfloat16)
    part_down = contract(upstream, hidden)
    grad_pre = (grad_hidden.astype(jnp.float32) * gelu_slope(pre_act)).astype(jnp.bfloat16)
    part_up = contract(normed, grad_pre)
    grad_normed = project_back(grad_pre, up_weight)
    grad_mixed = (
        upstream.astype(jnp.float32) + norm_rows_back(grad_normed, normal, inverse)
    ).astype(jnp.bfloat16)
    return (block_out, grad_mixed, part_up, part_down)


def attention_backward(
    token_lines, kept, padded_value, padded_grad, conv_kernel, qkv_weight, out_weight, mask_full
):
    qkv_rows, attended = kept
    grad_mixed = padded_grad[1:-1, 1:-1]
    grad_value = (
        grad_mixed.astype(jnp.float32) + conv_apply(padded_grad, conv_kernel[::-1, ::-1, ::-1])
    ).astype(jnp.bfloat16)
    part_kernel = kernel_grad(padded_value, grad_mixed)
    upstream = project_back(grad_value, out_weight).astype(jnp.bfloat16)
    part_out = contract(attended, grad_value)
    query_vec, key_vec, query_scale, key_scale, query_unit, key_unit, attn_probs, factor = (
        attention_parts(qkv_rows, mask_full, HEADS)
    )
    width = token_lines.shape[-1]
    value_heads = split_heads(qkv_rows[..., 2 * width :], HEADS)
    grad_heads = split_heads(upstream, HEADS)
    probs_low = attn_probs.astype(jnp.bfloat16)
    grad_probs = head_product("abihd,abjhd->abhij", grad_heads, value_heads)
    grad_values = head_product("abhij,abihd->abjhd", probs_low, grad_heads)
    grad_scores = attn_probs * (
        grad_probs - jnp.sum(grad_probs * attn_probs, axis=-1, keepdims=True)
    )
    grad_low = (factor * grad_scores).astype(jnp.bfloat16)
    grad_qunit = join_heads(
        head_product("abhij,abjhd->abihd", grad_low, split_heads(key_unit, HEADS))
    )
    grad_kunit = join_heads(
        head_product("abhij,abihd->abjhd", grad_low, split_heads(query_unit, HEADS))
    )
    grad_query = unit_back(grad_qunit, query_vec, query_scale).astype(jnp.bfloat16)
    grad_key = unit_back(grad_kunit, key_vec, key_scale).astype(jnp.bfloat16)
    grad_qkv = jnp.concatenate(
        [grad_query, grad_key, join_heads(grad_values).astype(jnp.bfloat16)], axis=-1
    )
    normal, inverse = norm_rows(token_lines.astype(jnp.float32))
    grad_normed = project_back(grad_qkv, qkv_weight).astype(jnp.bfloat16)
    part_qkv = contract(normal.astype(jnp.bfloat16), grad_qkv)
    token_gradient = (
        grad_value.astype(jnp.float32)
        + norm_rows_back(grad_normed.astype(jnp.float32), normal, inverse)
    ).astype(jnp.bfloat16)
    return token_gradient, jnp.concatenate([part_qkv, part_out], axis=1), part_kernel


def local(tokens, qkv_weight, out_weight, conv_kernel, up_weight, down_weight, band_mask, grad_out):
    count_y, count_z = lax.axis_size("gy"), lax.axis_size("gz")
    extent_x, part_y, part_z, width = tokens.shape
    planes = extent_x // count_y
    extents = (planes, part_y, part_z, width)
    block_count = band_mask.shape[0]
    line_length = block_count * BLOCK
    mask_full = (
        jnp.broadcast_to(band_mask[:, None, :, None], (block_count, BLOCK, block_count, BLOCK))
        .reshape(line_length, line_length)
        .astype(jnp.float32)
    )
    token_swapped, grad_swapped = swap_lines(
        tokens.reshape(count_y, -1, width), grad_out.reshape(count_y, -1, width), count_y
    )
    token_lines = to_lines(token_swapped, extents)
    grad_lines = to_lines(grad_swapped, extents)
    value_field, kept = attention_forward(token_lines, qkv_weight, out_weight, mask_full)
    padded_value = halo(value_field, count_y, count_z, 1)
    block_out, grad_mixed, part_up, part_down = feed_forward(
        padded_value, grad_lines, conv_kernel, up_weight, down_weight
    )
    padded_grad = halo(grad_mixed, count_y, count_z, 2)
    token_gradient, part_qkv_out, part_kernel = attention_backward(
        token_lines, kept, padded_value, padded_grad, conv_kernel, qkv_weight, out_weight, mask_full
    )
    hidden_width = up_weight.shape[1]
    pieces = [tiles_of(part_up), tiles_of(part_down), tiles_of(part_qkv_out)]
    kernel_flat = part_kernel.reshape(-1)
    kernel_tiles = -(-kernel_flat.shape[0] // 2048)
    used = sum(piece.shape[0] for piece in pieces)
    devices = count_y * count_z
    whole = -(-(used + kernel_tiles) // devices) * devices
    tail = jnp.pad(kernel_flat, (0, (whole - used) * 2048 - kernel_flat.shape[0]))
    parts = jnp.concatenate(pieces + [tail.reshape(-1, 16, 128)], axis=0)
    sums, block_swapped, token_swapped = reduce_and_swap(
        parts, from_lines(block_out, extents), from_lines(token_gradient, extents), count_y, count_z
    )
    factor = 1.0 / math.sqrt(extent_x * part_y * count_y * part_z * count_z)
    scaled = sums.astype(jnp.float32) * factor
    one = pieces[0].shape[0]
    up_sum = from_tiles(scaled[:one], width, hidden_width)
    down_sum = from_tiles(scaled[one : 2 * one], width, hidden_width).T
    joint = from_tiles(scaled[2 * one : used], width, 4 * width)
    kernel_sum = scaled[used:].reshape(-1)[: kernel_flat.shape[0]].reshape(conv_kernel.shape)
    return (
        block_swapped.reshape(tokens.shape),
        token_swapped.reshape(tokens.shape),
        joint[:, : 3 * width],
        joint[:, 3 * width :],
        kernel_sum,
        up_sum,
        down_sum,
    )


def solution(mesh):
    placed = (P(None, "gy", "gz", None), P(), P(), P(), P(), P(), P(), P(None, "gy", "gz", None))
    return jax.shard_map(
        local,
        mesh=mesh,
        in_specs=placed,
        out_specs=(P(None, "gy", "gz", None), P(None, "gy", "gz", None), P(), P(), P(), P(), P()),
        check_vma=False,
    )
```

```python
import functools
import math

import jax
import jax.numpy as jnp
from jax import lax
from jax.experimental import pallas as pl
from jax.experimental.pallas import tpu as pltpu
from jax.sharding import PartitionSpec as P

HEADS = 6
BLOCK = 16


NORM_EPS = 1e-05
UNIT_EPS = 1e-06
GELU_SLOPE = 0.7978845608028654
GELU_CUBIC = 0.044715


def norm_rows(values):
    centred = values - jnp.mean(values, axis=-1, keepdims=True)
    inverse = lax.rsqrt(jnp.mean(centred * centred, axis=-1, keepdims=True) + NORM_EPS)
    return (centred * inverse, inverse)


def norm_rows_back(upstream, normal, inverse):
    return inverse * (
        upstream
        - jnp.mean(upstream, axis=-1, keepdims=True)
        - normal * jnp.mean(upstream * normal, axis=-1, keepdims=True)
    )


def unit_scale(values):
    return lax.rsqrt(jnp.mean(values * values, axis=-1, keepdims=True) + UNIT_EPS)


def unit_back(upstream, values, scaling):
    return scaling * upstream - scaling * scaling * scaling * values * jnp.mean(
        upstream * values, axis=-1, keepdims=True
    )


MESH = pl.DeviceIdType.MESH
VMEM = pl.BlockSpec(memory_space=pltpu.VMEM)


def greet(peers):
    barrier = pltpu.get_barrier_semaphore()
    for peer in peers:
        pl.semaphore_signal(barrier, inc=1, device_id=peer, device_id_type=MESH)
    pl.semaphore_wait(barrier, len(peers))


def line_peers(count):
    me_y, me_z = lax.axis_index("gy"), lax.axis_index("gz")
    return [(lax.rem(me_y + k, count), me_z) for k in range(1, count)]


def swap_copies(count, pairs, send_sem, recv_sem):
    me_y, me_z = lax.axis_index("gy"), lax.axis_index("gz")
    copies = []
    for k in range(1, count):
        peer = lax.rem(me_y + k, count)
        for a, (source, target) in enumerate(pairs):
            copies.append(
                pltpu.make_async_remote_copy(
                    src_ref=source.at[peer],
                    dst_ref=target.at[me_y],
                    send_sem=send_sem.at[a, k],
                    recv_sem=recv_sem.at[a, k],
                    device_id=(peer, me_z),
                    device_id_type=MESH,
                )
            )
    return copies


def swap_kernel(count, first_in, second_in, first_out, second_out, send_sem, recv_sem):
    greet(line_peers(count))
    pairs = ((first_in, first_out), (second_in, second_out))
    copies = swap_copies(count, pairs, send_sem, recv_sem)
    for copy in copies:
        copy.start()
    me_y = lax.axis_index("gy")
    for source, target in pairs:
        target[me_y] = source[me_y]
    for copy in copies:
        copy.wait()


def swap_lines(first, second, count):
    shape = jax.ShapeDtypeStruct(first.shape, first.dtype)
    return pl.pallas_call(
        functools.partial(swap_kernel, count),
        out_shape=(shape, shape),
        in_specs=[VMEM, VMEM],
        out_specs=(VMEM, VMEM),
        scratch_shapes=[pltpu.SemaphoreType.DMA((2, count)), pltpu.SemaphoreType.DMA((2, count))],
        compiler_params=pltpu.CompilerParams(collective_id=0, has_side_effects=True),
        name="swap_lines",
    )(first, second)


def face(step, extent):
    return {0: (pl.ds(0, extent), pl.ds(1, extent)), 1: (pl.ds(extent - 1, 1), pl.ds(0, 1)), -1: (pl.ds(0, 1), pl.ds(extent + 1, 1))}[step]


def halo_kernel(count_y, count_z, cells, padded, send_sem, recv_sem):
    me_y, me_z = lax.axis_index("gy"), lax.axis_index("gz")
    extent_x, extent_z = cells.shape[0], cells.shape[1]
    steps = [(dx, dz) for dx in (-1, 0, 1) for dz in (-1, 0, 1) if (dx, dz) != (0, 0)]
    barrier = pltpu.get_barrier_semaphore()

    def reach(dx, action):
        if dx == 0:
            action()
        elif dx == 1:
            pl.when(me_y < count_y - 1)(action)
        else:
            pl.when(me_y > 0)(action)

    def place(dx, dz):
        return (me_y + dx, lax.rem(me_z + dz + count_z, count_z))

    def greet_one(dx, dz):
        pl.semaphore_signal(barrier, inc=1, device_id=place(dx, dz), device_id_type=MESH)

    for dx, dz in steps:
        reach(dx, functools.partial(greet_one, dx, dz))
    inner = (me_y > 0) & (me_y < count_y - 1)

    @pl.when(inner)
    def _():
        pl.semaphore_wait(barrier, 8)

    @pl.when(jnp.logical_not(inner))
    def _():
        pl.semaphore_wait(barrier, 5)

    def copy_of(index):
        dx, dz = steps[index]
        from_x, to_x = face(dx, extent_x)
        from_z, to_z = face(dz, extent_z)
        return pltpu.make_async_remote_copy(
            src_ref=cells.at[from_x, from_z],
            dst_ref=padded.at[to_x, to_z],
            send_sem=send_sem.at[index],
            recv_sem=recv_sem.at[index],
            device_id=place(dx, dz),
            device_id_type=MESH,
        )

    for index, (dx, dz) in enumerate(steps):
        reach(dx, lambda index=index: copy_of(index).start())
    padded[1 : extent_x + 1, 1 : extent_z + 1] = cells[...]
    blank = jnp.zeros((1,) + tuple(padded.shape[1:]), padded.dtype)

    @pl.when(me_y == 0)
    def _():
        padded[0:1] = blank

    @pl.when(me_y == count_y - 1)
    def _():
        padded[extent_x + 1 : extent_x + 2] = blank

    for index, (dx, dz) in enumerate(steps):
        reach(dx, lambda index=index: copy_of(index).wait_send())
        reach(-dx, lambda index=index: copy_of(index).wait_recv())


def halo(cells, count_y, count_z, number):
    shape = (cells.shape[0] + 2, cells.shape[1] + 2) + cells.shape[2:]
    return pl.pallas_call(
        functools.partial(halo_kernel, count_y, count_z),
        out_shape=jax.ShapeDtypeStruct(shape, cells.dtype),
        in_specs=[VMEM],
        out_specs=VMEM,
        scratch_shapes=[pltpu.SemaphoreType.DMA((8,)), pltpu.SemaphoreType.DMA((8,))],
        compiler_params=pltpu.CompilerParams(collective_id=number, has_side_effects=True),
        name="halo%d" % number,
    )(cells)


def bits_of(count_y, count_z):
    levels = []
    for axis, count in (("gz", count_z), ("gy", count_y)):
        bit = 1
        while bit < count:
            levels.append((axis, bit))
            bit *= 2
    return levels


def reduce_kernel(count_y, count_z, parts, first_in, second_in, sums, first_out, second_out, *scratch):
    swap_send, swap_recv, send_sem, recv_sem, total = scratch[:5]
    stages = bits_of(count_y, count_z)
    depth = len(stages)
    outgoing, incoming = scratch[5 : 5 + depth], scratch[5 + depth : 5 + 2 * depth]
    me = {"gy": lax.axis_index("gy"), "gz": lax.axis_index("gz")}
    bit_values, partners = [], []
    for axis, bit in stages:
        value = lax.rem(me[axis] // bit, 2)
        moved = me[axis] + bit * (1 - 2 * value)
        bit_values.append(value)
        partners.append((moved, me["gz"]) if axis == "gy" else (me["gy"], moved))
    greet(line_peers(count_y) + [partner for (axis, _), partner in zip(stages, partners) if axis == "gz"])
    pairs = ((first_in, first_out), (second_in, second_out))
    copies = swap_copies(count_y, pairs, swap_send, swap_recv)
    for copy in copies:
        copy.start()
    for source, target in pairs:
        target[me["gy"]] = source[me["gy"]]
    held, size = parts, parts.shape[0]
    base, bases = 0, []
    for level in range(depth):
        half = size // 2
        keep = base + bit_values[level] * half
        away = base + (1 - bit_values[level]) * half
        outgoing[level][...] = held[pl.ds(away, half)].astype(jnp.bfloat16)
        copy = pltpu.make_async_remote_copy(
            src_ref=outgoing[level],
            dst_ref=incoming[level],
            send_sem=send_sem.at[level],
            recv_sem=recv_sem.at[level],
            device_id=partners[level],
            device_id_type=MESH,
        )
        copy.start()
        copy.wait()
        total[pl.ds(keep, half)] = held[pl.ds(keep, half)] + incoming[level][...].astype(jnp.float32)
        held, base, size = total, keep, half
        bases.append(keep)
    sums[pl.ds(base, size)] = total[pl.ds(base, size)].astype(jnp.bfloat16)
    for level in range(depth - 1, -1, -1):
        span = pl.ds(bases[level], size)
        copy = pltpu.make_async_remote_copy(
            src_ref=sums.at[span],
            dst_ref=sums.at[span],
            send_sem=send_sem.at[depth + level],
            recv_sem=recv_sem.at[depth + level],
            device_id=partners[level],
            device_id_type=MESH,
        )
        copy.start()
        copy.wait()
        size *= 2
    for copy in copies:
        copy.wait()


def reduce_and_swap(parts, first, second, count_y, count_z):
    depth = len(bits_of(count_y, count_z))
    shape = jax.ShapeDtypeStruct(first.shape, first.dtype)
    halves = [
        pltpu.VMEM((parts.shape[0] >> (level + 1),) + parts.shape[1:], jnp.bfloat16)
        for level in range(depth)
    ]
    return pl.pallas_call(
        functools.partial(reduce_kernel, count_y, count_z),
        out_shape=(jax.ShapeDtypeStruct(parts.shape, jnp.bfloat16), shape, shape),
        in_specs=[VMEM, VMEM, VMEM],
        out_specs=(VMEM, VMEM, VMEM),
        scratch_shapes=[
            pltpu.SemaphoreType.DMA((2, count_y)),
            pltpu.SemaphoreType.DMA((2, count_y)),
            pltpu.SemaphoreType.DMA((2 * depth,)),
            pltpu.SemaphoreType.DMA((2 * depth,)),
            pltpu.VMEM(parts.shape, jnp.float32),
        ]
        + halves
        + halves,
        compiler_params=pltpu.CompilerParams(
            collective_id=3, has_side_effects=True, vmem_limit_bytes=24 * 1024 * 1024
        ),
        name="reduce_and_swap",
    )(parts, first, second)


def from_tiles(tiles, rows, columns):
    return (
        tiles.reshape(columns // 128, rows, 128)
        .transpose(1, 0, 2)
        .reshape(rows, columns)
    )


def to_lines(swapped, extents):
    planes, part_y, part_z, width = extents
    lines = swapped.reshape(-1, planes, part_y, part_z, width).transpose(1, 3, 0, 2, 4)
    return lines.reshape(planes, part_z, -1, width)


def from_lines(lines, extents):
    planes, part_y, part_z, width = extents
    split = lines.reshape(planes, part_z, -1, part_y, width).transpose(2, 0, 3, 1, 4)
    return split.reshape(split.shape[0], -1, width)

def dot(left, right, left_axis=1, right_axis=0):
    return lax.dot_general(
        left, right, (((left_axis,), (right_axis,)), ((), ())), preferred_element_type=jnp.float32
    )


def stack_heads(values):
    width = values.shape[1]
    head_of = lax.broadcasted_iota(jnp.int32, (1, width), 1) // (width // HEADS)
    return jnp.concatenate([jnp.where(head_of == h, values, 0.0) for h in range(HEADS)], axis=0)


def unstack_heads(stacked):
    rows, width = stacked.shape[0] // HEADS, stacked.shape[1]
    head_of = lax.broadcasted_iota(jnp.int32, (1, width), 1) // (width // HEADS)
    joined = stacked[:rows]
    for h in range(1, HEADS):
        joined = jnp.where(head_of == h, stacked[h * rows : (h + 1) * rows], joined)
    return joined


def line_probs(query_vec, key_vec, mask_stack):
    query_scale, key_scale = unit_scale(query_vec), unit_scale(key_vec)
    query_stack = stack_heads(query_vec * query_scale).astype(jnp.bfloat16)
    key_unit = (key_vec * key_scale).astype(jnp.bfloat16)
    factor = 2.0 / math.sqrt(query_vec.shape[1] // HEADS)
    weights = mask_stack * jnp.exp(factor * dot(query_stack, key_unit, 1, 1))
    probs = weights / jnp.sum(weights, axis=-1, keepdims=True)
    return query_scale, key_scale, query_stack, key_unit, probs, factor


def forward_kernel(tokens, qkv_weight, out_weight, mask, field, query, key, value, attended):
    planes, part_z, length, width = tokens.shape
    lines = planes * part_z
    token_wide = tokens[...].reshape(lines * length, width).astype(jnp.float32)
    normal, _ = norm_rows(token_wide)
    normed = normal.astype(jnp.bfloat16)
    for piece, target in enumerate((query, key, value)):
        weight = qkv_weight[:, piece * width : (piece + 1) * width]
        target[...] = dot(normed, weight).astype(jnp.bfloat16)
    for line in range(lines):
        rows = pl.ds(line * length, length)
        probs = line_probs(
            query[rows].astype(jnp.float32), key[rows].astype(jnp.float32), mask[...]
        )[4]
        attended[rows] = unstack_heads(dot(probs.astype(jnp.bfloat16), value[rows])).astype(
            jnp.bfloat16
        )
    field[...] = (
        (token_wide + dot(attended[...], out_weight[...])).astype(jnp.bfloat16).reshape(field.shape)
    )


def single(body, name, outs, scratch, *operands):
    return pl.pallas_call(
        body,
        out_shape=outs,
        in_specs=[VMEM] * len(operands),
        out_specs=[VMEM] * len(outs),
        scratch_shapes=scratch,
        compiler_params=pltpu.CompilerParams(vmem_limit_bytes=32 * 1024 * 1024),
        name=name,
    )(*operands)


def low(*shape):
    return jax.ShapeDtypeStruct(shape, jnp.bfloat16)


def wide(*shape):
    return jax.ShapeDtypeStruct(shape, jnp.float32)


def stacked_mask(mask_full):
    return jnp.tile(mask_full, (HEADS, 1))


def attention_forward(token_lines, qkv_weight, out_weight, mask_full):
    width = token_lines.shape[-1]
    count = token_lines.size // width
    flat = low(count, width)
    field, *kept = single(
        forward_kernel,
        "attention_forward",
        (low(*token_lines.shape), flat, flat, flat, flat),
        [],
        token_lines,
        qkv_weight,
        out_weight,
        stacked_mask(mask_full),
    )
    return field, kept


def shift_rows(values, step):
    return pltpu.roll(values, step % values.shape[0], 0)


def conv_line(padded, taps, plane, column):
    by_shift = [None, None, None]
    for a in range(3):
        for d in range(3):
            window = padded[plane + a, column + d].astype(jnp.float32)
            for b in range(3):
                tap = (a * 3 + b) * 3 + d
                term = taps[tap : tap + 1] * window
                by_shift[b] = term if by_shift[b] is None else by_shift[b] + term
    return shift_rows(by_shift[0], 1) + by_shift[1] + shift_rows(by_shift[2], -1)


def put_tiles(target, matrix):
    rows = matrix.shape[0] // 16
    for column in range(matrix.shape[1] // 128):
        target[column * rows : (column + 1) * rows] = matrix[
            :, column * 128 : (column + 1) * 128
        ].reshape(rows, 16, 128)


def mlp_kernel(
    padded, upstream, taps, up_weight, down_weight, block_out, grad_mixed, up_tiles, down_tiles,
    mixed, normed, hidden, grad_pre
):
    planes, part_z, length, width = upstream.shape
    for line in range(planes * part_z):
        plane, column = line // part_z, line % part_z
        rows = pl.ds(line * length, length)
        centre = padded[plane + 1, column + 1].astype(jnp.float32)
        mixed[rows] = (centre + conv_line(padded, taps, plane, column)).astype(jnp.bfloat16)
    group = min(2, part_z)
    for start in range(0, planes * part_z, group):
        plane, columns = start // part_z, pl.ds(start % part_z, group)
        rows = pl.ds(start * length, group * length)
        mixed_wide = mixed[rows].astype(jnp.float32)
        normal, inverse = norm_rows(mixed_wide)
        normed[rows] = normal.astype(jnp.bfloat16)
        pre_act = dot(normed[rows], up_weight[...])
        square = pre_act * pre_act
        tangent = jnp.tanh(GELU_SLOPE * (pre_act + GELU_CUBIC * square * pre_act))
        hidden[rows] = (0.5 * pre_act * (1.0 + tangent)).astype(jnp.bfloat16)
        slope = 0.5 * (1.0 + tangent) + 0.5 * pre_act * (1.0 - tangent * tangent) * GELU_SLOPE * (
            1.0 + 3.0 * GELU_CUBIC * square
        )
        above = upstream[plane, columns].reshape(group * length, width)
        grad_hidden = dot(above, down_weight[...], 1, 1).astype(jnp.bfloat16)
        grad_pre[rows] = (grad_hidden.astype(jnp.float32) * slope).astype(jnp.bfloat16)
        block_out[plane, columns] = (
            (mixed_wide + dot(hidden[rows], down_weight[...]))
            .astype(jnp.bfloat16)
            .reshape(group, length, width)
        )
        grad_normed = dot(grad_pre[rows], up_weight[...], 1, 1)
        grad_mixed[plane, columns] = (
            (above.astype(jnp.float32) + norm_rows_back(grad_normed, normal, inverse))
            .astype(jnp.bfloat16)
            .reshape(group, length, width)
        )
    put_tiles(up_tiles, dot(normed[...], grad_pre[...], 0, 0))
    put_tiles(down_tiles, dot(upstream[...].reshape(mixed.shape), hidden[...], 0, 0))


def feed_forward(padded_value, upstream, conv_kernel, up_weight, down_weight):
    width, hidden_width = up_weight.shape
    count = upstream.size // width
    tiles = wide(width * hidden_width // 2048, 16, 128)
    return single(
        mlp_kernel,
        "feed_forward",
        (low(*upstream.shape), low(*upstream.shape), tiles, tiles),
        [
            pltpu.VMEM((count, width), jnp.bfloat16),
            pltpu.VMEM((count, width), jnp.bfloat16),
            pltpu.VMEM((count, hidden_width), jnp.bfloat16),
            pltpu.VMEM((count, hidden_width), jnp.bfloat16),
        ],
        padded_value,
        upstream,
        conv_kernel.reshape(27, width),
        up_weight,
        down_weight,
    )


def backward_kernel(
    padded_value, padded_grad, tokens, query, key, value, attended, taps, qkv_weight, out_weight,
    mask, token_gradient, joint_tiles, tap_tiles, grad_value, above, grad_query, grad_key, grad_low_value,
    tap_sums
):
    planes, part_z, length, width = tokens.shape
    lines = planes * part_z
    tap_sums[...] = jnp.zeros_like(tap_sums)
    for line in range(lines):
        plane, column = line // part_z, line % part_z
        rows = pl.ds(line * length, length)
        centre = padded_grad[plane + 1, column + 1].astype(jnp.float32)
        grad_value[rows] = (centre + conv_line(padded_grad, taps, plane, column)).astype(jnp.bfloat16)
        shifted = (shift_rows(centre, -1), centre, shift_rows(centre, 1))
        for a in range(3):
            for d in range(3):
                window = padded_value[plane + a, column + d].astype(jnp.float32)
                for b in range(3):
                    product = (shifted[b] * window).reshape(length // 8, 8, width)
                    tap_sums[(a * 3 + b) * 3 + d] += jnp.sum(product, axis=0)
    above[...] = dot(grad_value[...], out_weight[...], 1, 1).astype(jnp.bfloat16)
    for line in range(lines):
        rows = pl.ds(line * length, length)
        query_vec, key_vec = query[rows].astype(jnp.float32), key[rows].astype(jnp.float32)
        query_scale, key_scale, query_stack, key_unit, probs, factor = line_probs(
            query_vec, key_vec, mask[...]
        )
        grad_stack = stack_heads(above[rows].astype(jnp.float32)).astype(jnp.bfloat16)
        grad_probs = dot(grad_stack, value[rows], 1, 1)
        grad_scores = probs * (grad_probs - jnp.sum(grad_probs * probs, axis=-1, keepdims=True))
        grad_low = (factor * grad_scores).astype(jnp.bfloat16)
        grad_low_value[rows] = dot(probs.astype(jnp.bfloat16), grad_stack, 0, 0).astype(jnp.bfloat16)
        grad_qunit = unstack_heads(dot(grad_low, key_unit))
        grad_kunit = dot(grad_low, query_stack, 0, 0)
        grad_query[rows] = unit_back(grad_qunit, query_vec, query_scale).astype(jnp.bfloat16)
        grad_key[rows] = unit_back(grad_kunit, key_vec, key_scale).astype(jnp.bfloat16)
    normal, inverse = norm_rows(tokens[...].reshape(lines * length, width).astype(jnp.float32))
    normed = normal.astype(jnp.bfloat16)
    grad_normed, parts = 0.0, []
    for piece, grad in enumerate((grad_query, grad_key, grad_low_value)):
        weight = qkv_weight[:, piece * width : (piece + 1) * width]
        grad_normed = grad_normed + dot(grad[...], weight, 1, 1)
        parts.append(dot(normed, grad[...], 0, 0))
    parts.append(dot(attended[...], grad_value[...], 0, 0))
    put_tiles(joint_tiles, jnp.concatenate(parts, axis=1))
    upstream = grad_normed.astype(jnp.bfloat16).astype(jnp.float32)
    token_gradient[...] = (
        (grad_value[...].astype(jnp.float32) + norm_rows_back(upstream, normal, inverse))
        .astype(jnp.bfloat16)
        .reshape(token_gradient.shape)
    )
    tap_tiles[...] = jnp.sum(tap_sums[...], axis=1)


def attention_backward(
    token_lines, kept, padded_value, padded_grad, conv_kernel, qkv_weight, out_weight, mask_full
):
    width = token_lines.shape[-1]
    count = token_lines.size // width
    return single(
        backward_kernel,
        "attention_backward",
        (low(*token_lines.shape), wide(4 * width * width // 2048, 16, 128), wide(27, width)),
        [pltpu.VMEM((count, width), jnp.bfloat16)] * 5 + [pltpu.VMEM((27, 8, width), jnp.float32)],
        padded_value,
        padded_grad,
        token_lines,
        *kept,
        conv_kernel[::-1, ::-1, ::-1].reshape(27, width),
        qkv_weight,
        out_weight,
        stacked_mask(mask_full),
    )


def local(tokens, qkv_weight, out_weight, conv_kernel, up_weight, down_weight, band_mask, grad_out):
    count_y, count_z = lax.axis_size("gy"), lax.axis_size("gz")
    extent_x, part_y, part_z, width = tokens.shape
    planes = extent_x // count_y
    extents = (planes, part_y, part_z, width)
    block_count = band_mask.shape[0]
    line_length = block_count * BLOCK
    mask_full = (
        jnp.broadcast_to(band_mask[:, None, :, None], (block_count, BLOCK, block_count, BLOCK))
        .reshape(line_length, line_length)
        .astype(jnp.float32)
    )
    token_swapped, grad_swapped = swap_lines(
        tokens.reshape(count_y, -1, width), grad_out.reshape(count_y, -1, width), count_y
    )
    token_lines = to_lines(token_swapped, extents)
    grad_lines = to_lines(grad_swapped, extents)
    value_field, kept = attention_forward(token_lines, qkv_weight, out_weight, mask_full)
    padded_value = halo(value_field, count_y, count_z, 1)
    block_out, grad_mixed, part_up, part_down = feed_forward(
        padded_value, grad_lines, conv_kernel, up_weight, down_weight
    )
    padded_grad = halo(grad_mixed, count_y, count_z, 2)
    token_gradient, part_qkv_out, part_kernel = attention_backward(
        token_lines, kept, padded_value, padded_grad, conv_kernel, qkv_weight, out_weight, mask_full
    )
    hidden_width = up_weight.shape[1]
    pieces = [part_up, part_down, part_qkv_out]
    kernel_flat = part_kernel.reshape(-1)
    kernel_tiles = -(-kernel_flat.shape[0] // 2048)
    used = sum(piece.shape[0] for piece in pieces)
    devices = count_y * count_z
    whole = -(-(used + kernel_tiles) // devices) * devices
    tail = jnp.pad(kernel_flat, (0, (whole - used) * 2048 - kernel_flat.shape[0]))
    parts = jnp.concatenate(pieces + [tail.reshape(-1, 16, 128)], axis=0)
    sums, block_swapped, token_swapped = reduce_and_swap(
        parts, from_lines(block_out, extents), from_lines(token_gradient, extents), count_y, count_z
    )
    factor = 1.0 / math.sqrt(extent_x * part_y * count_y * part_z * count_z)
    scaled = sums.astype(jnp.float32) * factor
    one = pieces[0].shape[0]
    up_sum = from_tiles(scaled[:one], width, hidden_width)
    down_sum = from_tiles(scaled[one : 2 * one], width, hidden_width).T
    joint = from_tiles(scaled[2 * one : used], width, 4 * width)
    kernel_sum = scaled[used:].reshape(-1)[: kernel_flat.shape[0]].reshape(conv_kernel.shape)
    return (
        block_swapped.reshape(tokens.shape),
        token_swapped.reshape(tokens.shape),
        joint[:, : 3 * width],
        joint[:, 3 * width :],
        kernel_sum,
        up_sum,
        down_sum,
    )


def solution(mesh):
    placed = (P(None, "gy", "gz", None), P(), P(), P(), P(), P(), P(), P(None, "gy", "gz", None))
    return jax.shard_map(
        local,
        mesh=mesh,
        in_specs=placed,
        out_specs=(P(None, "gy", "gz", None), P(None, "gy", "gz", None), P(), P(), P(), P(), P()),
        check_vma=False,
    )
```

```python
import functools
import math

import jax
import jax.numpy as jnp
from jax import lax
from jax.experimental import pallas as pl
from jax.experimental.pallas import tpu as pltpu
from jax.sharding import PartitionSpec as P

HEADS = 6
BLOCK = 16


NORM_EPS = 1e-05
UNIT_EPS = 1e-06
GELU_SLOPE = 0.7978845608028654
GELU_CUBIC = 0.044715


def norm_rows(values):
    centred = values - jnp.mean(values, axis=-1, keepdims=True)
    inverse = lax.rsqrt(jnp.mean(centred * centred, axis=-1, keepdims=True) + NORM_EPS)
    return (centred * inverse, inverse)


def norm_rows_back(upstream, normal, inverse):
    return inverse * (
        upstream
        - jnp.mean(upstream, axis=-1, keepdims=True)
        - normal * jnp.mean(upstream * normal, axis=-1, keepdims=True)
    )


def unit_scale(values):
    return lax.rsqrt(jnp.mean(values * values, axis=-1, keepdims=True) + UNIT_EPS)


def unit_back(upstream, values, scaling):
    return scaling * upstream - scaling * scaling * scaling * values * jnp.mean(
        upstream * values, axis=-1, keepdims=True
    )


MESH = pl.DeviceIdType.MESH
VMEM = pl.BlockSpec(memory_space=pltpu.VMEM)


def greet(peers):
    barrier = pltpu.get_barrier_semaphore()
    for peer in peers:
        pl.semaphore_signal(barrier, inc=1, device_id=peer, device_id_type=MESH)
    pl.semaphore_wait(barrier, len(peers))


def line_peers(count):
    me_y, me_z = lax.axis_index("gy"), lax.axis_index("gz")
    return [(lax.rem(me_y + k, count), me_z) for k in range(1, count)]


def place_of(index):
    return index + (1 - 2 * lax.rem(index, 2)) * lax.rem(index // 2, 2)


def swap_copies(count, pairs, send_sem, recv_sem, inward):
    me_y, me_z = lax.axis_index("gy"), lax.axis_index("gz")
    copies = []
    for k in range(1, count):
        peer = lax.rem(me_y + k, count)
        for a, (source, target) in enumerate(pairs):
            copies.append(
                pltpu.make_async_remote_copy(
                    src_ref=source.at[place_of(peer) if inward else peer],
                    dst_ref=target.at[me_y if inward else place_of(me_y)],
                    send_sem=send_sem.at[a, k],
                    recv_sem=recv_sem.at[a, k],
                    device_id=(peer, me_z),
                    device_id_type=MESH,
                )
            )
    return copies


def swap_kernel(count, first_in, second_in, first_out, second_out, send_sem, recv_sem):
    greet(line_peers(count))
    pairs = ((first_in, first_out), (second_in, second_out))
    copies = swap_copies(count, pairs, send_sem, recv_sem, True)
    for copy in copies:
        copy.start()
    me_y = lax.axis_index("gy")
    for source, target in pairs:
        target[me_y] = source[place_of(me_y)]
    for copy in copies:
        copy.wait()


def swap_lines(first, second, count):
    shape = jax.ShapeDtypeStruct(first.shape, first.dtype)
    return pl.pallas_call(
        functools.partial(swap_kernel, count),
        out_shape=(shape, shape),
        in_specs=[VMEM, VMEM],
        out_specs=(VMEM, VMEM),
        scratch_shapes=[pltpu.SemaphoreType.DMA((2, count)), pltpu.SemaphoreType.DMA((2, count))],
        compiler_params=pltpu.CompilerParams(collective_id=0, has_side_effects=True),
        name="swap_lines",
    )(first, second)


def face(step, extent):
    return {0: (pl.ds(0, extent), pl.ds(1, extent)), 1: (pl.ds(extent - 1, 1), pl.ds(0, 1)), -1: (pl.ds(0, 1), pl.ds(extent + 1, 1))}[step]


def halo_kernel(count_y, count_z, cells, padded, send_sem, recv_sem):
    me_y, me_z = place_of(lax.axis_index("gy")), lax.axis_index("gz")
    extent_x, extent_z = cells.shape[0], cells.shape[1]
    steps = [(dx, dz) for dx in (-1, 0, 1) for dz in (-1, 0, 1) if (dx, dz) != (0, 0)]
    barrier = pltpu.get_barrier_semaphore()

    def reach(dx, action):
        if dx == 0:
            action()
        elif dx == 1:
            pl.when(me_y < count_y - 1)(action)
        else:
            pl.when(me_y > 0)(action)

    def place(dx, dz):
        return (place_of(me_y + dx), lax.rem(me_z + dz + count_z, count_z))

    def greet_one(dx, dz):
        pl.semaphore_signal(barrier, inc=1, device_id=place(dx, dz), device_id_type=MESH)

    for dx, dz in steps:
        reach(dx, functools.partial(greet_one, dx, dz))
    inner = (me_y > 0) & (me_y < count_y - 1)

    @pl.when(inner)
    def _():
        pl.semaphore_wait(barrier, 8)

    @pl.when(jnp.logical_not(inner))
    def _():
        pl.semaphore_wait(barrier, 5)

    def copy_of(index):
        dx, dz = steps[index]
        from_x, to_x = face(dx, extent_x)
        from_z, to_z = face(dz, extent_z)
        return pltpu.make_async_remote_copy(
            src_ref=cells.at[from_x, from_z],
            dst_ref=padded.at[to_x, to_z],
            send_sem=send_sem.at[index],
            recv_sem=recv_sem.at[index],
            device_id=place(dx, dz),
            device_id_type=MESH,
        )

    for index, (dx, dz) in enumerate(steps):
        reach(dx, lambda index=index: copy_of(index).start())
    padded[1 : extent_x + 1, 1 : extent_z + 1] = cells[...]
    blank = jnp.zeros((1,) + tuple(padded.shape[1:]), padded.dtype)

    @pl.when(me_y == 0)
    def _():
        padded[0:1] = blank

    @pl.when(me_y == count_y - 1)
    def _():
        padded[extent_x + 1 : extent_x + 2] = blank

    for index, (dx, dz) in enumerate(steps):
        reach(dx, lambda index=index: copy_of(index).wait_send())
        reach(-dx, lambda index=index: copy_of(index).wait_recv())


def halo(cells, count_y, count_z, number):
    shape = (cells.shape[0] + 2, cells.shape[1] + 2) + cells.shape[2:]
    return pl.pallas_call(
        functools.partial(halo_kernel, count_y, count_z),
        out_shape=jax.ShapeDtypeStruct(shape, cells.dtype),
        in_specs=[VMEM],
        out_specs=VMEM,
        scratch_shapes=[pltpu.SemaphoreType.DMA((8,)), pltpu.SemaphoreType.DMA((8,))],
        compiler_params=pltpu.CompilerParams(collective_id=number, has_side_effects=True),
        name="halo%d" % number,
    )(cells)


def bits_of(count):
    return [1 << level for level in range(count.bit_length() - 1)]


def reduce_kernel(
    count_y, count_z, chains, parts, first_in, second_in, sums, first_out, second_out, *scratch
):
    swap_send, swap_recv, send_sem, recv_sem, total = scratch[:5]
    buffers = scratch[5:]
    bits = bits_of(count_z)
    depth = len(bits)
    me_y, me_z = lax.axis_index("gy"), lax.axis_index("gz")
    values = [lax.rem(me_z // bit, 2) for bit in bits]
    partners = [(me_y, me_z + bit * (1 - 2 * value)) for bit, value in zip(bits, values)]
    greet(line_peers(count_y) + partners)
    pairs = ((first_in, first_out), (second_in, second_out))
    copies = swap_copies(count_y, pairs, swap_send, swap_recv, False)

    def send(source, target, chain, slot, peer):
        copy = pltpu.make_async_remote_copy(
            src_ref=source,
            dst_ref=target,
            send_sem=send_sem.at[chain, slot],
            recv_sem=recv_sem.at[chain, slot],
            device_id=peer,
            device_id_type=MESH,
        )
        copy.start()
        return copy

    def run_chain(chain):
        base, size = chains[chain]
        mine = buffers[chain * (2 * depth + 2) : (chain + 1) * (2 * depth + 2)]
        outgoing, incoming = mine[: depth + 1], mine[depth + 1 :]
        held, bases = parts, []
        for level in range(depth):
            half = size // 2
            keep = base + values[level] * half
            away = base + (1 - values[level]) * half
            outgoing[level][...] = held[pl.ds(away, half)].astype(jnp.bfloat16)
            copy = send(outgoing[level], incoming[level], chain, level, partners[level])
            yield
            copy.wait()
            total[pl.ds(keep, half)] = held[pl.ds(keep, half)] + incoming[level][...].astype(
                jnp.float32
            )
            held, base, size = total, keep, half
            bases.append(keep)
        part = size // count_y
        outgoing[depth][...] = held[pl.ds(base, size)].astype(jnp.bfloat16)
        spread = []
        for k in range(1, count_y):
            peer = lax.rem(me_y + k, count_y)
            source = outgoing[depth].at[pl.ds(peer * part, part)]
            spread.append(
                send(source, incoming[depth].at[k], chain, 2 * depth + k, (peer, me_z))
            )
        yield
        own = pl.ds(base + me_y * part, part)
        summed = held[own]
        for k, copy in enumerate(spread):
            copy.wait()
            summed = summed + incoming[depth][k + 1].astype(jnp.float32)
        sums[own] = summed.astype(jnp.bfloat16)
        spread = []
        for k in range(1, count_y):
            peer = lax.rem(me_y + k, count_y)
            spread.append(
                send(sums.at[own], sums.at[own], chain, 2 * depth + count_y + k, (peer, me_z))
            )
        yield
        for copy in spread:
            copy.wait()
        for level in range(depth - 1, -1, -1):
            span = pl.ds(bases[level], size)
            copy = send(sums.at[span], sums.at[span], chain, depth + level, partners[level])
            yield
            copy.wait()
            size *= 2

    running = [run_chain(chain) for chain in range(len(chains))]
    first_round = True
    while running:
        still = []
        for work in running:
            if next(work, "done") is None:
                still.append(work)
        running = still
        if first_round:
            for copy in copies:
                copy.start()
            for source, target in pairs:
                target[place_of(me_y)] = source[me_y]
            first_round = False
    for copy in copies:
        copy.wait()


def reduce_and_swap(parts, first, second, count_y, count_z):
    depth = len(bits_of(count_z))
    shape = jax.ShapeDtypeStruct(first.shape, first.dtype)
    units = parts.shape[0] // (count_y * count_z)
    chain_count = min(3, units)
    cuts = [i * units // chain_count * count_y * count_z for i in range(chain_count + 1)]
    chains = [(low_cut, high_cut - low_cut) for low_cut, high_cut in zip(cuts, cuts[1:])]
    tile = parts.shape[1:]
    buffers = []
    for _, size in chains:
        halves = [(size >> (level + 1),) + tile for level in range(depth)]
        last = size >> depth
        shapes = halves + [(last,) + tile] + halves + [(count_y, last // count_y) + tile]
        buffers += [pltpu.VMEM(entry, jnp.bfloat16) for entry in shapes]
    slots = (chain_count, 2 * depth + 2 * count_y)
    return pl.pallas_call(
        functools.partial(reduce_kernel, count_y, count_z, chains),
        out_shape=(jax.ShapeDtypeStruct(parts.shape, jnp.bfloat16), shape, shape),
        in_specs=[VMEM, VMEM, VMEM],
        out_specs=(VMEM, VMEM, VMEM),
        scratch_shapes=[
            pltpu.SemaphoreType.DMA((2, count_y)),
            pltpu.SemaphoreType.DMA((2, count_y)),
            pltpu.SemaphoreType.DMA(slots),
            pltpu.SemaphoreType.DMA(slots),
            pltpu.VMEM(parts.shape, jnp.float32),
        ]
        + buffers,
        compiler_params=pltpu.CompilerParams(
            collective_id=3, has_side_effects=True, vmem_limit_bytes=60 * 1024 * 1024
        ),
        name="reduce_and_swap",
    )(parts, first, second)


def from_tiles(tiles, rows, columns):
    return (
        tiles.reshape(columns // 128, rows, 128)
        .transpose(1, 0, 2)
        .reshape(rows, columns)
    )


def to_lines(swapped, extents):
    planes, part_y, part_z, width = extents
    lines = swapped.reshape(-1, planes, part_y, part_z, width).transpose(1, 3, 0, 2, 4)
    return lines.reshape(planes, part_z, -1, width)


def from_lines(lines, extents):
    planes, part_y, part_z, width = extents
    split = lines.reshape(planes, part_z, -1, part_y, width).transpose(2, 0, 3, 1, 4)
    return split.reshape(split.shape[0], -1, width)

def dot(left, right, left_axis=1, right_axis=0):
    return lax.dot_general(
        left, right, (((left_axis,), (right_axis,)), ((), ())), preferred_element_type=jnp.float32
    )


def stack_heads(values):
    width = values.shape[1]
    head_of = lax.broadcasted_iota(jnp.int32, (1, width), 1) // (width // HEADS)
    return jnp.concatenate([jnp.where(head_of == h, values, 0.0) for h in range(HEADS)], axis=0)


def unstack_heads(stacked):
    rows, width = stacked.shape[0] // HEADS, stacked.shape[1]
    head_of = lax.broadcasted_iota(jnp.int32, (1, width), 1) // (width // HEADS)
    joined = stacked[:rows]
    for h in range(1, HEADS):
        joined = jnp.where(head_of == h, stacked[h * rows : (h + 1) * rows], joined)
    return joined


def line_probs(query_vec, key_vec, mask_stack):
    query_scale, key_scale = unit_scale(query_vec), unit_scale(key_vec)
    query_stack = stack_heads(query_vec * query_scale).astype(jnp.bfloat16)
    key_unit = (key_vec * key_scale).astype(jnp.bfloat16)
    factor = 2.0 / math.sqrt(query_vec.shape[1] // HEADS)
    weights = mask_stack * jnp.exp(factor * dot(query_stack, key_unit, 1, 1))
    probs = weights / jnp.sum(weights, axis=-1, keepdims=True)
    return query_scale, key_scale, query_stack, key_unit, probs, factor


def forward_kernel(tokens, qkv_weight, out_weight, mask, field, query, key, value, attended):
    planes, part_z, length, width = tokens.shape
    lines = planes * part_z
    token_wide = tokens[...].reshape(lines * length, width).astype(jnp.float32)
    normal, _ = norm_rows(token_wide)
    normed = normal.astype(jnp.bfloat16)
    for piece, target in enumerate((query, key, value)):
        weight = qkv_weight[:, piece * width : (piece + 1) * width]
        target[...] = dot(normed, weight).astype(jnp.bfloat16)
    for line in range(lines):
        rows = pl.ds(line * length, length)
        probs = line_probs(
            query[rows].astype(jnp.float32), key[rows].astype(jnp.float32), mask[...]
        )[4]
        attended[rows] = unstack_heads(dot(probs.astype(jnp.bfloat16), value[rows])).astype(
            jnp.bfloat16
        )
    field[...] = (
        (token_wide + dot(attended[...], out_weight[...])).astype(jnp.bfloat16).reshape(field.shape)
    )


def single(body, name, outs, scratch, *operands):
    return pl.pallas_call(
        body,
        out_shape=outs,
        in_specs=[VMEM] * len(operands),
        out_specs=[VMEM] * len(outs),
        scratch_shapes=scratch,
        compiler_params=pltpu.CompilerParams(vmem_limit_bytes=60 * 1024 * 1024),
        name=name,
    )(*operands)


def low(*shape):
    return jax.ShapeDtypeStruct(shape, jnp.bfloat16)


def wide(*shape):
    return jax.ShapeDtypeStruct(shape, jnp.float32)


def stacked_mask(mask_full):
    return jnp.tile(mask_full, (HEADS, 1))


def attention_forward(token_lines, qkv_weight, out_weight, mask_full):
    width = token_lines.shape[-1]
    count = token_lines.size // width
    flat = low(count, width)
    field, *kept = single(
        forward_kernel,
        "attention_forward",
        (low(*token_lines.shape), flat, flat, flat, flat),
        [],
        token_lines,
        qkv_weight,
        out_weight,
        stacked_mask(mask_full),
    )
    return field, kept


def shift_rows(values, step):
    return pltpu.roll(values, step % values.shape[0], 0)


def conv_line(padded, taps, plane, column):
    by_shift = [None, None, None]
    for a in range(3):
        for d in range(3):
            window = padded[plane + a, column + d].astype(jnp.float32)
            for b in range(3):
                tap = (a * 3 + b) * 3 + d
                term = taps[tap : tap + 1] * window
                by_shift[b] = term if by_shift[b] is None else by_shift[b] + term
    return shift_rows(by_shift[0], 1) + by_shift[1] + shift_rows(by_shift[2], -1)


def put_tiles(target, matrix):
    rows = matrix.shape[0] // 16
    for column in range(matrix.shape[1] // 128):
        target[column * rows : (column + 1) * rows] = matrix[
            :, column * 128 : (column + 1) * 128
        ].reshape(rows, 16, 128)


def mlp_kernel(
    padded, upstream, taps, up_weight, down_weight, block_out, grad_mixed, up_tiles, down_tiles,
    mixed, normed, hidden, grad_pre
):
    planes, part_z, length, width = upstream.shape
    for line in range(planes * part_z):
        plane, column = line // part_z, line % part_z
        rows = pl.ds(line * length, length)
        centre = padded[plane + 1, column + 1].astype(jnp.float32)
        mixed[rows] = (centre + conv_line(padded, taps, plane, column)).astype(jnp.bfloat16)
    group = min(2, part_z)
    for start in range(0, planes * part_z, group):
        plane, columns = start // part_z, pl.ds(start % part_z, group)
        rows = pl.ds(start * length, group * length)
        mixed_wide = mixed[rows].astype(jnp.float32)
        normal, inverse = norm_rows(mixed_wide)
        normed[rows] = normal.astype(jnp.bfloat16)
        pre_act = dot(normed[rows], up_weight[...])
        square = pre_act * pre_act
        tangent = jnp.tanh(GELU_SLOPE * (pre_act + GELU_CUBIC * square * pre_act))
        hidden[rows] = (0.5 * pre_act * (1.0 + tangent)).astype(jnp.bfloat16)
        slope = 0.5 * (1.0 + tangent) + 0.5 * pre_act * (1.0 - tangent * tangent) * GELU_SLOPE * (
            1.0 + 3.0 * GELU_CUBIC * square
        )
        above = upstream[plane, columns].reshape(group * length, width)
        grad_hidden = dot(above, down_weight[...], 1, 1).astype(jnp.bfloat16)
        grad_pre[rows] = (grad_hidden.astype(jnp.float32) * slope).astype(jnp.bfloat16)
        block_out[plane, columns] = (
            (mixed_wide + dot(hidden[rows], down_weight[...]))
            .astype(jnp.bfloat16)
            .reshape(group, length, width)
        )
        grad_normed = dot(grad_pre[rows], up_weight[...], 1, 1)
        grad_mixed[plane, columns] = (
            (above.astype(jnp.float32) + norm_rows_back(grad_normed, normal, inverse))
            .astype(jnp.bfloat16)
            .reshape(group, length, width)
        )
    put_tiles(up_tiles, dot(normed[...], grad_pre[...], 0, 0))
    put_tiles(down_tiles, dot(upstream[...].reshape(mixed.shape), hidden[...], 0, 0))


def feed_forward(padded_value, upstream, conv_kernel, up_weight, down_weight):
    width, hidden_width = up_weight.shape
    count = upstream.size // width
    tiles = wide(width * hidden_width // 2048, 16, 128)
    return single(
        mlp_kernel,
        "feed_forward",
        (low(*upstream.shape), low(*upstream.shape), tiles, tiles),
        [
            pltpu.VMEM((count, width), jnp.bfloat16),
            pltpu.VMEM((count, width), jnp.bfloat16),
            pltpu.VMEM((count, hidden_width), jnp.bfloat16),
            pltpu.VMEM((count, hidden_width), jnp.bfloat16),
        ],
        padded_value,
        upstream,
        conv_kernel.reshape(27, width),
        up_weight,
        down_weight,
    )


def backward_kernel(
    padded_value, padded_grad, tokens, query, key, value, attended, taps, qkv_weight, out_weight,
    mask, token_gradient, joint_tiles, tap_tiles, grad_value, above, grad_query, grad_key, grad_low_value,
    tap_sums
):
    planes, part_z, length, width = tokens.shape
    lines = planes * part_z
    tap_sums[...] = jnp.zeros_like(tap_sums)
    for line in range(lines):
        plane, column = line // part_z, line % part_z
        rows = pl.ds(line * length, length)
        centre = padded_grad[plane + 1, column + 1].astype(jnp.float32)
        grad_value[rows] = (centre + conv_line(padded_grad, taps, plane, column)).astype(jnp.bfloat16)
        shifted = (shift_rows(centre, -1), centre, shift_rows(centre, 1))
        for a in range(3):
            for d in range(3):
                window = padded_value[plane + a, column + d].astype(jnp.float32)
                for b in range(3):
                    product = (shifted[b] * window).reshape(length // 8, 8, width)
                    tap_sums[(a * 3 + b) * 3 + d] += jnp.sum(product, axis=0)
    above[...] = dot(grad_value[...], out_weight[...], 1, 1).astype(jnp.bfloat16)
    for line in range(lines):
        rows = pl.ds(line * length, length)
        query_vec, key_vec = query[rows].astype(jnp.float32), key[rows].astype(jnp.float32)
        query_scale, key_scale, query_stack, key_unit, probs, factor = line_probs(
            query_vec, key_vec, mask[...]
        )
        grad_stack = stack_heads(above[rows].astype(jnp.float32)).astype(jnp.bfloat16)
        grad_probs = dot(grad_stack, value[rows], 1, 1)
        grad_scores = probs * (grad_probs - jnp.sum(grad_probs * probs, axis=-1, keepdims=True))
        grad_low = (factor * grad_scores).astype(jnp.bfloat16)
        grad_low_value[rows] = dot(probs.astype(jnp.bfloat16), grad_stack, 0, 0).astype(jnp.bfloat16)
        grad_qunit = unstack_heads(dot(grad_low, key_unit))
        grad_kunit = dot(grad_low, query_stack, 0, 0)
        grad_query[rows] = unit_back(grad_qunit, query_vec, query_scale).astype(jnp.bfloat16)
        grad_key[rows] = unit_back(grad_kunit, key_vec, key_scale).astype(jnp.bfloat16)
    normal, inverse = norm_rows(tokens[...].reshape(lines * length, width).astype(jnp.float32))
    normed = normal.astype(jnp.bfloat16)
    grad_normed, parts = 0.0, []
    for piece, grad in enumerate((grad_query, grad_key, grad_low_value)):
        weight = qkv_weight[:, piece * width : (piece + 1) * width]
        grad_normed = grad_normed + dot(grad[...], weight, 1, 1)
        parts.append(dot(normed, grad[...], 0, 0))
    parts.append(dot(attended[...], grad_value[...], 0, 0))
    put_tiles(joint_tiles, jnp.concatenate(parts, axis=1))
    upstream = grad_normed.astype(jnp.bfloat16).astype(jnp.float32)
    token_gradient[...] = (
        (grad_value[...].astype(jnp.float32) + norm_rows_back(upstream, normal, inverse))
        .astype(jnp.bfloat16)
        .reshape(token_gradient.shape)
    )
    tap_tiles[...] = jnp.sum(tap_sums[...], axis=1)


def attention_backward(
    token_lines, kept, padded_value, padded_grad, conv_kernel, qkv_weight, out_weight, mask_full
):
    width = token_lines.shape[-1]
    count = token_lines.size // width
    return single(
        backward_kernel,
        "attention_backward",
        (low(*token_lines.shape), wide(4 * width * width // 2048, 16, 128), wide(27, width)),
        [pltpu.VMEM((count, width), jnp.bfloat16)] * 5 + [pltpu.VMEM((27, 8, width), jnp.float32)],
        padded_value,
        padded_grad,
        token_lines,
        *kept,
        conv_kernel[::-1, ::-1, ::-1].reshape(27, width),
        qkv_weight,
        out_weight,
        stacked_mask(mask_full),
    )


def local(tokens, qkv_weight, out_weight, conv_kernel, up_weight, down_weight, band_mask, grad_out):
    count_y, count_z = lax.axis_size("gy"), lax.axis_size("gz")
    extent_x, part_y, part_z, width = tokens.shape
    planes = extent_x // count_y
    extents = (planes, part_y, part_z, width)
    block_count = band_mask.shape[0]
    line_length = block_count * BLOCK
    mask_full = (
        jnp.broadcast_to(band_mask[:, None, :, None], (block_count, BLOCK, block_count, BLOCK))
        .reshape(line_length, line_length)
        .astype(jnp.float32)
    )
    token_swapped, grad_swapped = swap_lines(
        tokens.reshape(count_y, -1, width), grad_out.reshape(count_y, -1, width), count_y
    )
    token_lines = to_lines(token_swapped, extents)
    grad_lines = to_lines(grad_swapped, extents)
    value_field, kept = attention_forward(token_lines, qkv_weight, out_weight, mask_full)
    padded_value = halo(value_field, count_y, count_z, 1)
    block_out, grad_mixed, part_up, part_down = feed_forward(
        padded_value, grad_lines, conv_kernel, up_weight, down_weight
    )
    padded_grad = halo(grad_mixed, count_y, count_z, 2)
    token_gradient, part_qkv_out, part_kernel = attention_backward(
        token_lines, kept, padded_value, padded_grad, conv_kernel, qkv_weight, out_weight, mask_full
    )
    hidden_width = up_weight.shape[1]
    pieces = [part_up, part_down, part_qkv_out]
    kernel_flat = part_kernel.reshape(-1)
    kernel_tiles = -(-kernel_flat.shape[0] // 2048)
    used = sum(piece.shape[0] for piece in pieces)
    devices = count_y * count_z
    whole = -(-(used + kernel_tiles) // devices) * devices
    tail = jnp.pad(kernel_flat, (0, (whole - used) * 2048 - kernel_flat.shape[0]))
    parts = jnp.concatenate(pieces + [tail.reshape(-1, 16, 128)], axis=0)
    sums, block_swapped, token_swapped = reduce_and_swap(
        parts, from_lines(block_out, extents), from_lines(token_gradient, extents), count_y, count_z
    )
    factor = 1.0 / math.sqrt(extent_x * part_y * count_y * part_z * count_z)
    scaled = sums.astype(jnp.float32) * factor
    one = pieces[0].shape[0]
    up_sum = from_tiles(scaled[:one], width, hidden_width)
    down_sum = from_tiles(scaled[one : 2 * one], width, hidden_width).T
    joint = from_tiles(scaled[2 * one : used], width, 4 * width)
    kernel_sum = scaled[used:].reshape(-1)[: kernel_flat.shape[0]].reshape(conv_kernel.shape)
    return (
        block_swapped.reshape(tokens.shape),
        token_swapped.reshape(tokens.shape),
        joint[:, : 3 * width],
        joint[:, 3 * width :],
        kernel_sum,
        up_sum,
        down_sum,
    )


def solution(mesh):
    placed = (P(None, "gy", "gz", None), P(), P(), P(), P(), P(), P(), P(None, "gy", "gz", None))
    return jax.shard_map(
        local,
        mesh=mesh,
        in_specs=placed,
        out_specs=(P(None, "gy", "gz", None), P(None, "gy", "gz", None), P(), P(), P(), P(), P()),
        check_vma=False,
    )
```

```python
import functools
import math

import jax
import jax.numpy as jnp
from jax import lax
from jax.experimental import pallas as pl
from jax.experimental.pallas import tpu as pltpu
from jax.sharding import PartitionSpec as P

HEADS = 6
BLOCK = 16


NORM_EPS = 1e-05
UNIT_EPS = 1e-06
GELU_SLOPE = 0.7978845608028654
GELU_CUBIC = 0.044715


def norm_rows(values):
    centred = values - jnp.mean(values, axis=-1, keepdims=True)
    inverse = lax.rsqrt(jnp.mean(centred * centred, axis=-1, keepdims=True) + NORM_EPS)
    return (centred * inverse, inverse)


def norm_rows_back(upstream, normal, inverse):
    return inverse * (
        upstream
        - jnp.mean(upstream, axis=-1, keepdims=True)
        - normal * jnp.mean(upstream * normal, axis=-1, keepdims=True)
    )


def unit_scale(values):
    return lax.rsqrt(jnp.mean(values * values, axis=-1, keepdims=True) + UNIT_EPS)


def unit_back(upstream, values, scaling):
    return scaling * upstream - scaling * scaling * scaling * values * jnp.mean(
        upstream * values, axis=-1, keepdims=True
    )


MESH = pl.DeviceIdType.MESH
VMEM = pl.BlockSpec(memory_space=pltpu.VMEM)


def greet(peers):
    barrier = pltpu.get_barrier_semaphore()
    for peer in peers:
        pl.semaphore_signal(barrier, inc=1, device_id=peer, device_id_type=MESH)
    pl.semaphore_wait(barrier, len(peers))


def line_peers(count):
    me_y, me_z = lax.axis_index("gy"), lax.axis_index("gz")
    return [(lax.rem(me_y + k, count), me_z) for k in range(1, count)]


def place_of(index):
    return index + (1 - 2 * lax.rem(index, 2)) * lax.rem(index // 2, 2)


def swap_copies(count, pairs, send_sem, recv_sem, inward):
    me_y, me_z = lax.axis_index("gy"), lax.axis_index("gz")
    copies = []
    for k in range(1, count):
        peer = lax.rem(me_y + k, count)
        for a, (source, target) in enumerate(pairs):
            copies.append(
                pltpu.make_async_remote_copy(
                    src_ref=source.at[place_of(peer) if inward else peer],
                    dst_ref=target.at[me_y if inward else place_of(me_y)],
                    send_sem=send_sem.at[a, k],
                    recv_sem=recv_sem.at[a, k],
                    device_id=(peer, me_z),
                    device_id_type=MESH,
                )
            )
    return copies


def swap_kernel(count, first_in, second_in, first_out, second_out, send_sem, recv_sem):
    greet(line_peers(count))
    pairs = ((first_in, first_out), (second_in, second_out))
    copies = swap_copies(count, pairs, send_sem, recv_sem, True)
    for copy in copies:
        copy.start()
    me_y = lax.axis_index("gy")
    for source, target in pairs:
        target[me_y] = source[place_of(me_y)]
    for copy in copies:
        copy.wait()


def swap_lines(first, second, count):
    shape = jax.ShapeDtypeStruct(first.shape, first.dtype)
    return pl.pallas_call(
        functools.partial(swap_kernel, count),
        out_shape=(shape, shape),
        in_specs=[VMEM, VMEM],
        out_specs=(VMEM, VMEM),
        scratch_shapes=[pltpu.SemaphoreType.DMA((2, count)), pltpu.SemaphoreType.DMA((2, count))],
        compiler_params=pltpu.CompilerParams(collective_id=0, has_side_effects=True),
        name="swap_lines",
    )(first, second)


def face(step, extent):
    return {0: (pl.ds(0, extent), pl.ds(1, extent)), 1: (pl.ds(extent - 1, 1), pl.ds(0, 1)), -1: (pl.ds(0, 1), pl.ds(extent + 1, 1))}[step]


def halo_kernel(count_y, count_z, cells, padded, send_sem, recv_sem):
    me_y, me_z = place_of(lax.axis_index("gy")), lax.axis_index("gz")
    extent_x, extent_z = cells.shape[0], cells.shape[1]
    steps = [(dx, dz) for dx in (-1, 0, 1) for dz in (-1, 0, 1) if (dx, dz) != (0, 0)]
    barrier = pltpu.get_barrier_semaphore()

    def reach(dx, action):
        if dx == 0:
            action()
        elif dx == 1:
            pl.when(me_y < count_y - 1)(action)
        else:
            pl.when(me_y > 0)(action)

    def place(dx, dz):
        return (place_of(me_y + dx), lax.rem(me_z + dz + count_z, count_z))

    def greet_one(dx, dz):
        pl.semaphore_signal(barrier, inc=1, device_id=place(dx, dz), device_id_type=MESH)

    for dx, dz in steps:
        reach(dx, functools.partial(greet_one, dx, dz))
    inner = (me_y > 0) & (me_y < count_y - 1)

    @pl.when(inner)
    def _():
        pl.semaphore_wait(barrier, 8)

    @pl.when(jnp.logical_not(inner))
    def _():
        pl.semaphore_wait(barrier, 5)

    def copy_of(index):
        dx, dz = steps[index]
        from_x, to_x = face(dx, extent_x)
        from_z, to_z = face(dz, extent_z)
        return pltpu.make_async_remote_copy(
            src_ref=cells.at[from_x, from_z],
            dst_ref=padded.at[to_x, to_z],
            send_sem=send_sem.at[index],
            recv_sem=recv_sem.at[index],
            device_id=place(dx, dz),
            device_id_type=MESH,
        )

    for index, (dx, dz) in enumerate(steps):
        reach(dx, lambda index=index: copy_of(index).start())
    padded[1 : extent_x + 1, 1 : extent_z + 1] = cells[...]
    blank = jnp.zeros((1,) + tuple(padded.shape[1:]), padded.dtype)

    @pl.when(me_y == 0)
    def _():
        padded[0:1] = blank

    @pl.when(me_y == count_y - 1)
    def _():
        padded[extent_x + 1 : extent_x + 2] = blank

    for index, (dx, dz) in enumerate(steps):
        reach(dx, lambda index=index: copy_of(index).wait_send())
        reach(-dx, lambda index=index: copy_of(index).wait_recv())


def halo(cells, count_y, count_z, number):
    shape = (cells.shape[0] + 2, cells.shape[1] + 2) + cells.shape[2:]
    return pl.pallas_call(
        functools.partial(halo_kernel, count_y, count_z),
        out_shape=jax.ShapeDtypeStruct(shape, cells.dtype),
        in_specs=[VMEM],
        out_specs=VMEM,
        scratch_shapes=[pltpu.SemaphoreType.DMA((8,)), pltpu.SemaphoreType.DMA((8,))],
        compiler_params=pltpu.CompilerParams(collective_id=number, has_side_effects=True),
        name="halo%d" % number,
    )(cells)


def bits_of(count):
    return [1 << level for level in range(count.bit_length() - 1)]


def reduce_kernel(
    count_y, count_z, chains, parts, first_in, second_in, sums, first_out, second_out, *scratch
):
    swap_send, swap_recv, send_sem, recv_sem, total = scratch[:5]
    buffers = scratch[5:]
    bits = bits_of(count_z)
    depth = len(bits)
    me_y, me_z = lax.axis_index("gy"), lax.axis_index("gz")
    values = [lax.rem(me_z // bit, 2) for bit in bits]
    partners = [(me_y, me_z + bit * (1 - 2 * value)) for bit, value in zip(bits, values)]
    greet(line_peers(count_y) + partners)
    pairs = ((first_in, first_out), (second_in, second_out))
    copies = swap_copies(count_y, pairs, swap_send, swap_recv, False)

    def send(source, target, chain, slot, peer):
        copy = pltpu.make_async_remote_copy(
            src_ref=source,
            dst_ref=target,
            send_sem=send_sem.at[chain, slot],
            recv_sem=recv_sem.at[chain, slot],
            device_id=peer,
            device_id_type=MESH,
        )
        copy.start()
        return copy

    def run_chain(chain):
        base, size = chains[chain]
        mine = buffers[chain * (2 * depth + 2) : (chain + 1) * (2 * depth + 2)]
        outgoing, incoming = mine[: depth + 1], mine[depth + 1 :]
        held, bases = parts, []
        for level in range(depth):
            half = size // 2
            keep = base + values[level] * half
            away = base + (1 - values[level]) * half
            outgoing[level][...] = held[pl.ds(away, half)].astype(jnp.bfloat16)
            copy = send(outgoing[level], incoming[level], chain, level, partners[level])
            yield
            copy.wait()
            total[pl.ds(keep, half)] = held[pl.ds(keep, half)] + incoming[level][...].astype(
                jnp.float32
            )
            held, base, size = total, keep, half
            bases.append(keep)
        part = size // count_y
        outgoing[depth][...] = held[pl.ds(base, size)].astype(jnp.bfloat16)
        spread = []
        for k in range(1, count_y):
            peer = lax.rem(me_y + k, count_y)
            source = outgoing[depth].at[pl.ds(peer * part, part)]
            spread.append(
                send(source, incoming[depth].at[k], chain, 2 * depth + k, (peer, me_z))
            )
        yield
        own = pl.ds(base + me_y * part, part)
        summed = held[own]
        for k, copy in enumerate(spread):
            copy.wait()
            summed = summed + incoming[depth][k + 1].astype(jnp.float32)
        sums[own] = summed.astype(jnp.bfloat16)
        spread = []
        for k in range(1, count_y):
            peer = lax.rem(me_y + k, count_y)
            spread.append(
                send(sums.at[own], sums.at[own], chain, 2 * depth + count_y + k, (peer, me_z))
            )
        yield
        for copy in spread:
            copy.wait()
        for level in range(depth - 1, -1, -1):
            span = pl.ds(bases[level], size)
            copy = send(sums.at[span], sums.at[span], chain, depth + level, partners[level])
            yield
            copy.wait()
            size *= 2

    running = [run_chain(chain) for chain in range(len(chains))]
    first_round = True
    while running:
        still = []
        for work in running:
            if next(work, "done") is None:
                still.append(work)
        running = still
        if first_round:
            for copy in copies:
                copy.start()
            for source, target in pairs:
                target[place_of(me_y)] = source[me_y]
            first_round = False
    for copy in copies:
        copy.wait()


def reduce_and_swap(parts, first, second, count_y, count_z):
    depth = len(bits_of(count_z))
    shape = jax.ShapeDtypeStruct(first.shape, first.dtype)
    units = parts.shape[0] // (count_y * count_z)
    chain_count = min(3, units)
    cuts = [i * units // chain_count * count_y * count_z for i in range(chain_count + 1)]
    chains = [(low_cut, high_cut - low_cut) for low_cut, high_cut in zip(cuts, cuts[1:])]
    tile = parts.shape[1:]
    buffers = []
    for _, size in chains:
        halves = [(size >> (level + 1),) + tile for level in range(depth)]
        last = size >> depth
        shapes = halves + [(last,) + tile] + halves + [(count_y, last // count_y) + tile]
        buffers += [pltpu.VMEM(entry, jnp.bfloat16) for entry in shapes]
    slots = (chain_count, 2 * depth + 2 * count_y)
    return pl.pallas_call(
        functools.partial(reduce_kernel, count_y, count_z, chains),
        out_shape=(jax.ShapeDtypeStruct(parts.shape, jnp.bfloat16), shape, shape),
        in_specs=[VMEM, VMEM, VMEM],
        out_specs=(VMEM, VMEM, VMEM),
        scratch_shapes=[
            pltpu.SemaphoreType.DMA((2, count_y)),
            pltpu.SemaphoreType.DMA((2, count_y)),
            pltpu.SemaphoreType.DMA(slots),
            pltpu.SemaphoreType.DMA(slots),
            pltpu.VMEM(parts.shape, jnp.float32),
        ]
        + buffers,
        compiler_params=pltpu.CompilerParams(
            collective_id=3, has_side_effects=True, vmem_limit_bytes=24 * 1024 * 1024
        ),
        name="reduce_and_swap",
    )(parts, first, second)


def from_tiles(tiles, rows, columns):
    return (
        tiles.reshape(columns // 128, rows, 128)
        .transpose(1, 0, 2)
        .reshape(rows, columns)
    )


def to_lines(swapped, extents):
    planes, part_y, part_z, width = extents
    lines = swapped.reshape(-1, planes, part_y, part_z, width).transpose(1, 3, 0, 2, 4)
    return lines.reshape(planes, part_z, -1, width)


def from_lines(lines, extents):
    planes, part_y, part_z, width = extents
    split = lines.reshape(planes, part_z, -1, part_y, width).transpose(2, 0, 3, 1, 4)
    return split.reshape(split.shape[0], -1, width)

def dot(left, right, left_axis=1, right_axis=0):
    return lax.dot_general(
        left, right, (((left_axis,), (right_axis,)), ((), ())), preferred_element_type=jnp.float32
    )


def stack_heads(values):
    width = values.shape[1]
    head_of = lax.broadcasted_iota(jnp.int32, (1, width), 1) // (width // HEADS)
    return jnp.concatenate([jnp.where(head_of == h, values, 0.0) for h in range(HEADS)], axis=0)


def unstack_heads(stacked):
    rows, width = stacked.shape[0] // HEADS, stacked.shape[1]
    head_of = lax.broadcasted_iota(jnp.int32, (1, width), 1) // (width // HEADS)
    joined = stacked[:rows]
    for h in range(1, HEADS):
        joined = jnp.where(head_of == h, stacked[h * rows : (h + 1) * rows], joined)
    return joined


def line_probs(query_vec, key_vec, mask_stack):
    query_scale, key_scale = unit_scale(query_vec), unit_scale(key_vec)
    query_stack = stack_heads(query_vec * query_scale).astype(jnp.bfloat16)
    key_unit = (key_vec * key_scale).astype(jnp.bfloat16)
    factor = 2.0 / math.sqrt(query_vec.shape[1] // HEADS)
    weights = mask_stack * jnp.exp(factor * dot(query_stack, key_unit, 1, 1))
    probs = weights / jnp.sum(weights, axis=-1, keepdims=True)
    return query_scale, key_scale, query_stack, key_unit, probs, factor


def forward_kernel(tokens, qkv_weight, out_weight, mask, field, query, key, value, attended):
    planes, part_z, length, width = tokens.shape
    lines = planes * part_z
    token_wide = tokens[...].reshape(lines * length, width).astype(jnp.float32)
    normal, _ = norm_rows(token_wide)
    normed = normal.astype(jnp.bfloat16)
    for piece, target in enumerate((query, key, value)):
        weight = qkv_weight[:, piece * width : (piece + 1) * width]
        target[...] = dot(normed, weight).astype(jnp.bfloat16)
    for line in range(lines):
        rows = pl.ds(line * length, length)
        probs = line_probs(
            query[rows].astype(jnp.float32), key[rows].astype(jnp.float32), mask[...]
        )[4]
        attended[rows] = unstack_heads(dot(probs.astype(jnp.bfloat16), value[rows])).astype(
            jnp.bfloat16
        )
    field[...] = (
        (token_wide + dot(attended[...], out_weight[...])).astype(jnp.bfloat16).reshape(field.shape)
    )


def single(body, name, outs, scratch, *operands):
    return pl.pallas_call(
        body,
        out_shape=outs,
        in_specs=[VMEM] * len(operands),
        out_specs=[VMEM] * len(outs),
        scratch_shapes=scratch,
        compiler_params=pltpu.CompilerParams(vmem_limit_bytes=32 * 1024 * 1024),
        name=name,
    )(*operands)


def low(*shape):
    return jax.ShapeDtypeStruct(shape, jnp.bfloat16)


def wide(*shape):
    return jax.ShapeDtypeStruct(shape, jnp.float32)


def stacked_mask(mask_full):
    return jnp.tile(mask_full, (HEADS, 1))


def attention_forward(token_lines, qkv_weight, out_weight, mask_full):
    width = token_lines.shape[-1]
    count = token_lines.size // width
    flat = low(count, width)
    field, *kept = single(
        forward_kernel,
        "attention_forward",
        (low(*token_lines.shape), flat, flat, flat, flat),
        [],
        token_lines,
        qkv_weight,
        out_weight,
        stacked_mask(mask_full),
    )
    return field, kept


def shift_rows(values, step):
    return pltpu.roll(values, step % values.shape[0], 0)


def conv_line(padded, taps, plane, column):
    by_shift = [None, None, None]
    for a in range(3):
        for d in range(3):
            window = padded[plane + a, column + d].astype(jnp.float32)
            for b in range(3):
                tap = (a * 3 + b) * 3 + d
                term = taps[tap : tap + 1] * window
                by_shift[b] = term if by_shift[b] is None else by_shift[b] + term
    return shift_rows(by_shift[0], 1) + by_shift[1] + shift_rows(by_shift[2], -1)


def put_tiles(target, matrix):
    rows = matrix.shape[0] // 16
    for column in range(matrix.shape[1] // 128):
        target[column * rows : (column + 1) * rows] = matrix[
            :, column * 128 : (column + 1) * 128
        ].reshape(rows, 16, 128)


def mlp_kernel(
    padded, upstream, taps, up_weight, down_weight, block_out, grad_mixed, up_tiles, down_tiles,
    mixed, normed, hidden, grad_pre
):
    planes, part_z, length, width = upstream.shape
    for line in range(planes * part_z):
        plane, column = line // part_z, line % part_z
        rows = pl.ds(line * length, length)
        centre = padded[plane + 1, column + 1].astype(jnp.float32)
        mixed[rows] = (centre + conv_line(padded, taps, plane, column)).astype(jnp.bfloat16)
    group = min(2, part_z)
    for start in range(0, planes * part_z, group):
        plane, columns = start // part_z, pl.ds(start % part_z, group)
        rows = pl.ds(start * length, group * length)
        mixed_wide = mixed[rows].astype(jnp.float32)
        normal, inverse = norm_rows(mixed_wide)
        normed[rows] = normal.astype(jnp.bfloat16)
        pre_act = dot(normed[rows], up_weight[...])
        square = pre_act * pre_act
        tangent = jnp.tanh(GELU_SLOPE * (pre_act + GELU_CUBIC * square * pre_act))
        hidden[rows] = (0.5 * pre_act * (1.0 + tangent)).astype(jnp.bfloat16)
        slope = 0.5 * (1.0 + tangent) + 0.5 * pre_act * (1.0 - tangent * tangent) * GELU_SLOPE * (
            1.0 + 3.0 * GELU_CUBIC * square
        )
        above = upstream[plane, columns].reshape(group * length, width)
        grad_hidden = dot(above, down_weight[...], 1, 1).astype(jnp.bfloat16)
        grad_pre[rows] = (grad_hidden.astype(jnp.float32) * slope).astype(jnp.bfloat16)
        block_out[plane, columns] = (
            (mixed_wide + dot(hidden[rows], down_weight[...]))
            .astype(jnp.bfloat16)
            .reshape(group, length, width)
        )
        grad_normed = dot(grad_pre[rows], up_weight[...], 1, 1)
        grad_mixed[plane, columns] = (
            (above.astype(jnp.float32) + norm_rows_back(grad_normed, normal, inverse))
            .astype(jnp.bfloat16)
            .reshape(group, length, width)
        )
    put_tiles(up_tiles, dot(normed[...], grad_pre[...], 0, 0))
    put_tiles(down_tiles, dot(upstream[...].reshape(mixed.shape), hidden[...], 0, 0))


def feed_forward(padded_value, upstream, conv_kernel, up_weight, down_weight):
    width, hidden_width = up_weight.shape
    count = upstream.size // width
    tiles = wide(width * hidden_width // 2048, 16, 128)
    return single(
        mlp_kernel,
        "feed_forward",
        (low(*upstream.shape), low(*upstream.shape), tiles, tiles),
        [
            pltpu.VMEM((count, width), jnp.bfloat16),
            pltpu.VMEM((count, width), jnp.bfloat16),
            pltpu.VMEM((count, hidden_width), jnp.bfloat16),
            pltpu.VMEM((count, hidden_width), jnp.bfloat16),
        ],
        padded_value,
        upstream,
        conv_kernel.reshape(27, width),
        up_weight,
        down_weight,
    )


def backward_kernel(
    padded_value, padded_grad, tokens, query, key, value, attended, taps, qkv_weight, out_weight,
    mask, token_gradient, joint_tiles, tap_tiles, grad_value, above, grad_query, grad_key, grad_low_value,
    tap_sums
):
    planes, part_z, length, width = tokens.shape
    lines = planes * part_z
    tap_sums[...] = jnp.zeros_like(tap_sums)
    for line in range(lines):
        plane, column = line // part_z, line % part_z
        rows = pl.ds(line * length, length)
        centre = padded_grad[plane + 1, column + 1].astype(jnp.float32)
        grad_value[rows] = (centre + conv_line(padded_grad, taps, plane, column)).astype(jnp.bfloat16)
        shifted = (shift_rows(centre, -1), centre, shift_rows(centre, 1))
        for a in range(3):
            for d in range(3):
                window = padded_value[plane + a, column + d].astype(jnp.float32)
                for b in range(3):
                    product = (shifted[b] * window).reshape(length // 8, 8, width)
                    tap_sums[(a * 3 + b) * 3 + d] += jnp.sum(product, axis=0)
    above[...] = dot(grad_value[...], out_weight[...], 1, 1).astype(jnp.bfloat16)
    for line in range(lines):
        rows = pl.ds(line * length, length)
        query_vec, key_vec = query[rows].astype(jnp.float32), key[rows].astype(jnp.float32)
        query_scale, key_scale, query_stack, key_unit, probs, factor = line_probs(
            query_vec, key_vec, mask[...]
        )
        grad_stack = stack_heads(above[rows].astype(jnp.float32)).astype(jnp.bfloat16)
        grad_probs = dot(grad_stack, value[rows], 1, 1)
        grad_scores = probs * (grad_probs - jnp.sum(grad_probs * probs, axis=-1, keepdims=True))
        grad_low = (factor * grad_scores).astype(jnp.bfloat16)
        grad_low_value[rows] = dot(probs.astype(jnp.bfloat16), grad_stack, 0, 0).astype(jnp.bfloat16)
        grad_qunit = unstack_heads(dot(grad_low, key_unit))
        grad_kunit = dot(grad_low, query_stack, 0, 0)
        grad_query[rows] = unit_back(grad_qunit, query_vec, query_scale).astype(jnp.bfloat16)
        grad_key[rows] = unit_back(grad_kunit, key_vec, key_scale).astype(jnp.bfloat16)
    normal, inverse = norm_rows(tokens[...].reshape(lines * length, width).astype(jnp.float32))
    normed = normal.astype(jnp.bfloat16)
    grad_normed, parts = 0.0, []
    for piece, grad in enumerate((grad_query, grad_key, grad_low_value)):
        weight = qkv_weight[:, piece * width : (piece + 1) * width]
        grad_normed = grad_normed + dot(grad[...], weight, 1, 1)
        parts.append(dot(normed, grad[...], 0, 0))
    parts.append(dot(attended[...], grad_value[...], 0, 0))
    put_tiles(joint_tiles, jnp.concatenate(parts, axis=1))
    upstream = grad_normed.astype(jnp.bfloat16).astype(jnp.float32)
    token_gradient[...] = (
        (grad_value[...].astype(jnp.float32) + norm_rows_back(upstream, normal, inverse))
        .astype(jnp.bfloat16)
        .reshape(token_gradient.shape)
    )
    tap_tiles[...] = jnp.sum(tap_sums[...], axis=1)


def attention_backward(
    token_lines, kept, padded_value, padded_grad, conv_kernel, qkv_weight, out_weight, mask_full
):
    width = token_lines.shape[-1]
    count = token_lines.size // width
    return single(
        backward_kernel,
        "attention_backward",
        (low(*token_lines.shape), wide(4 * width * width // 2048, 16, 128), wide(27, width)),
        [pltpu.VMEM((count, width), jnp.bfloat16)] * 5 + [pltpu.VMEM((27, 8, width), jnp.float32)],
        padded_value,
        padded_grad,
        token_lines,
        *kept,
        conv_kernel[::-1, ::-1, ::-1].reshape(27, width),
        qkv_weight,
        out_weight,
        stacked_mask(mask_full),
    )


def local(tokens, qkv_weight, out_weight, conv_kernel, up_weight, down_weight, band_mask, grad_out):
    count_y, count_z = lax.axis_size("gy"), lax.axis_size("gz")
    extent_x, part_y, part_z, width = tokens.shape
    planes = extent_x // count_y
    extents = (planes, part_y, part_z, width)
    block_count = band_mask.shape[0]
    line_length = block_count * BLOCK
    mask_full = (
        jnp.broadcast_to(band_mask[:, None, :, None], (block_count, BLOCK, block_count, BLOCK))
        .reshape(line_length, line_length)
        .astype(jnp.float32)
    )
    token_swapped, grad_swapped = swap_lines(
        tokens.reshape(count_y, -1, width), grad_out.reshape(count_y, -1, width), count_y
    )
    token_lines = to_lines(token_swapped, extents)
    grad_lines = to_lines(grad_swapped, extents)
    value_field, kept = attention_forward(token_lines, qkv_weight, out_weight, mask_full)
    padded_value = halo(value_field, count_y, count_z, 1)
    block_out, grad_mixed, part_up, part_down = feed_forward(
        padded_value, grad_lines, conv_kernel, up_weight, down_weight
    )
    padded_grad = halo(grad_mixed, count_y, count_z, 2)
    token_gradient, part_qkv_out, part_kernel = attention_backward(
        token_lines, kept, padded_value, padded_grad, conv_kernel, qkv_weight, out_weight, mask_full
    )
    hidden_width = up_weight.shape[1]
    pieces = [part_up, part_down, part_qkv_out]
    kernel_flat = part_kernel.reshape(-1)
    kernel_tiles = -(-kernel_flat.shape[0] // 2048)
    used = sum(piece.shape[0] for piece in pieces)
    devices = count_y * count_z
    whole = -(-(used + kernel_tiles) // devices) * devices
    tail = jnp.pad(kernel_flat, (0, (whole - used) * 2048 - kernel_flat.shape[0]))
    parts = jnp.concatenate(pieces + [tail.reshape(-1, 16, 128)], axis=0)
    sums, block_swapped, token_swapped = reduce_and_swap(
        parts, from_lines(block_out, extents), from_lines(token_gradient, extents), count_y, count_z
    )
    factor = 1.0 / math.sqrt(extent_x * part_y * count_y * part_z * count_z)
    scaled = sums.astype(jnp.float32) * factor
    one = pieces[0].shape[0]
    up_sum = from_tiles(scaled[:one], width, hidden_width)
    down_sum = from_tiles(scaled[one : 2 * one], width, hidden_width).T
    joint = from_tiles(scaled[2 * one : used], width, 4 * width)
    kernel_sum = scaled[used:].reshape(-1)[: kernel_flat.shape[0]].reshape(conv_kernel.shape)
    return (
        block_swapped.reshape(tokens.shape),
        token_swapped.reshape(tokens.shape),
        joint[:, : 3 * width],
        joint[:, 3 * width :],
        kernel_sum,
        up_sum,
        down_sum,
    )


def solution(mesh):
    placed = (P(None, "gy", "gz", None), P(), P(), P(), P(), P(), P(), P(None, "gy", "gz", None))
    return jax.shard_map(
        local,
        mesh=mesh,
        in_specs=placed,
        out_specs=(P(None, "gy", "gz", None), P(None, "gy", "gz", None), P(), P(), P(), P(), P()),
        check_vma=False,
    )
```
